32 devices in a mesh: grp: 2 (over y), tau: 16 (over z, x, core).
Axes of the slice: x: 2, y: 2, z: 4, core: 2. Of those that a mesh axis runs over, the one named last changes fastest.
Arguments:
- propagator: float32 [4096, 36864], P(('grp', 'tau')), parts along dimension 0, may hold values from -2.4 to 2.4, as said below
- onsite_coupling: float32 [2], P('grp'), parts along dimension 0, may hold values from 2 to 4
- neighbour_strength: float32 [2], P('grp'), parts along dimension 0, may hold values from 0.3 to 1
Outputs:
- self_energy: float32 [4096, 36864], P(('grp', 'tau')), parts along dimension 0
The draws below stay inside these ranges and needn't reach their ends.
There are 2 independent parts, one for each index of `grp`. The reference program is written for one: setup_inputs(seed, part) draws one part's arguments, and reference() takes and returns one part's arrays. A program takes and returns all parts, laid end to end along the dimension named above; each array names one. Nothing has to cross between parts.
Inputs may be any that keep to these rules, and one draw needn't show every extreme that they name: propagator is even in the lattice vector: propagator[t, x * 192 + y] equals propagator[t, ((-x) mod 192) * 192 + ((-y) mod 192)].
All inputs are finite; a program needn't handle non-finite values.
Results may differ from the reference program's by a relative error of at most 0.00016.
Values sent between devices are 32-bit elements; how exact they have to be, the bound alone decides.
No kernel may reach another device: no remote copies, remote signals or barrier semaphores. Data moves between devices by JAX's collectives and lax.ppermute only.
A program may use at most 256 MiB of HBM per device.

```python
import math
import jax
import jax.numpy as jnp
from jax import lax

L = 192
TAU_POINTS = 2048
NF = 1024


def reflect_sites(values):
    return jnp.roll(jnp.flip(values, (1, 2)), 1, axis=(1, 2))


def draw_propagator(key, part):
    base = jax.random.truncated_normal(key, -4.0, 4.0, (TAU_POINTS, L, L), jnp.float32)
    values = 0.6 * (0.5 * (base + reflect_sites(base)))
    return values.reshape(TAU_POINTS, L * L).astype(jnp.float32)


def setup_inputs(seed: int = 0, part: int = 0) -> dict:
    arg_keys = jax.random.split(jax.random.key(seed), 4)
    own_keys = jax.random.split(jax.random.fold_in(arg_keys[3], part), 4)
    return {
        "propagator": draw_propagator(jax.random.fold_in(jax.random.fold_in(arg_keys[3], part), 71), part),
        "onsite_coupling": jnp.clip(jax.random.uniform(own_keys[1], (1,), jnp.float32, 2.0, 4.0), 2.0, 4.0),
        "neighbour_strength": jnp.clip(jax.random.uniform(own_keys[2], (1,), jnp.float32, 0.3, 1.0), 0.3, 1.0),
    }


largest_mode = lax.Precision.HIGHEST

def time_tables():
    matsubara_frequency = jnp.arange(NF, dtype=jnp.int32)[:, None]
    time_points = jnp.arange(TAU_POINTS, dtype=jnp.int32)[None, :]
    fourier_phase = matsubara_frequency * (2 * time_points + 1) % (2 * TAU_POINTS)
    forward = jnp.cos(jnp.pi * fourier_phase.astype(jnp.float32) / TAU_POINTS) / math.sqrt(TAU_POINTS)
    inverse = forward * jnp.where(matsubara_frequency == 0, 1.0, 2.0).astype(jnp.float32)
    return (forward, inverse)

def space_tables():
    waves = jnp.arange(L, dtype=jnp.int32)
    fourier_phase = waves[:, None] * waves[None, :] % L
    angle = 2.0 * jnp.pi * fourier_phase.astype(jnp.float32) / L
    return (jnp.cos(angle) / math.sqrt(L), jnp.sin(angle) / math.sqrt(L))

def spatial_transform(field, cosine, sine_table):
    first_cos = jnp.einsum('kx,fxy->fky', cosine, field, precision=largest_mode)
    first_sin = jnp.einsum('kx,fxy->fky', sine_table, field, precision=largest_mode)
    return jnp.einsum('fky,ly->fkl', first_cos, cosine, precision=largest_mode) - jnp.einsum('fky,ly->fkl', first_sin, sine_table, precision=largest_mode)

def bare_potential(indices, onsite, nearest):
    first = (indices // L).astype(jnp.float32)
    second = (indices % L).astype(jnp.float32)
    return onsite + 2.0 * nearest * (jnp.cos(2.0 * jnp.pi * first / L) + jnp.cos(2.0 * jnp.pi * second / L))

def screen(pol_mom, bare):
    denom = jnp.maximum(1.0 - bare * pol_mom, 1.0)
    return bare * bare * pol_mom / denom

def reference(propagator, onsite_coupling, neighbour_strength):
    forward, inverse = time_tables()
    cosine, sine_table = space_tables()
    polarization = -propagator * propagator[::-1]
    pol_freq = jnp.dot(forward, polarization, precision=largest_mode)
    pol_mom = spatial_transform(pol_freq.reshape(NF, L, L), cosine, sine_table).reshape(NF, L * L)
    bare = bare_potential(jnp.arange(L * L, dtype=jnp.int32), onsite_coupling[0], neighbour_strength[0])
    screened = screen(pol_mom, bare[None, :])
    back = spatial_transform(screened.reshape(NF, L, L), cosine, sine_table).reshape(NF, L * L)
    w_time = jnp.dot(inverse.T, back, precision=largest_mode)
    return -propagator * w_time
```

```python
import math

import jax
import jax.numpy as jnp
import numpy as np
from jax import lax
from jax.experimental import pallas as pl
from jax.experimental.pallas import tpu as pltpu
from jax.sharding import PartitionSpec as P

L = 192
TAU_POINTS = 2048
NF = 1024

mode = lax.Precision.HIGH


def cos_table(rows, columns, period):
    phase = rows[:, None] * columns[None, :] % period
    return jnp.cos(2.0 * jnp.pi * phase.astype(jnp.float32) / period)


def sin_table(rows, columns, period):
    phase = rows[:, None] * columns[None, :] % period
    return jnp.sin(2.0 * jnp.pi * phase.astype(jnp.float32) / period)


def time_table(times, points):
    frequency = jnp.arange(NF, dtype=jnp.int32)[None, :]
    phase = frequency * (2 * times[:, None] + 1) % (2 * points)
    return jnp.cos(jnp.pi * phase.astype(jnp.float32) / points) / math.sqrt(points)


def bare_potential(first, second, onsite, nearest):
    first = first.astype(jnp.float32)
    second = second.astype(jnp.float32)
    return onsite + 2.0 * nearest * (
        jnp.cos(2.0 * jnp.pi * first / L) + jnp.cos(2.0 * jnp.pi * second / L)
    )


def screen(pol_mom, bare):
    denom = jnp.maximum(1.0 - bare * pol_mom, 1.0)
    return bare * bare * pol_mom / denom


def plain(propagator, onsite_coupling, neighbour_strength):
    devices = lax.axis_size("tau")
    slab, sites = propagator.shape
    half = slab // 2
    points = slab * devices
    kept = L // 2 + 1
    width = kept * L
    block = -(-width // (8 * devices)) * 8
    padded = block * devices

    waves = jnp.arange(L, dtype=jnp.int32)
    halves = jnp.arange(kept, dtype=jnp.int32)
    twice = jnp.where((halves == 0) | (halves == L // 2), 1.0, 2.0).astype(jnp.float32)

    partner = [(d, devices - 1 - d) for d in range(devices)]
    mirrored = lax.ppermute(propagator[half:, :width], "tau", partner)
    polarization = -propagator[:half, :width] * mirrored[::-1]

    field = polarization.reshape(half, kept, L)
    along_cos = cos_table(halves, waves, L) / L
    along_sin = sin_table(halves, waves, L) / L
    first_cos = jnp.einsum("fxy,ly->fxl", field, along_cos, precision=mode)
    first_sin = jnp.einsum("fxy,ly->fxl", field, along_sin, precision=mode)
    cos_x = cos_table(waves, halves, L)
    sin_x = sin_table(waves, halves, L)
    pol_mom = jnp.einsum("fxl,kx->flk", first_cos, cos_x * twice, precision=mode) - jnp.einsum(
        "fxl,kx->flk", first_sin, sin_x * twice, precision=mode
    )
    pol_mom = jnp.pad(pol_mom.reshape(half, width), ((0, 0), (0, padded - width)))
    by_momentum = lax.all_to_all(pol_mom, "tau", split_axis=1, concat_axis=0, tiled=True)

    held = jnp.arange(devices * half, dtype=jnp.int32)
    times = held // half * slab + held % half
    forward = 2.0 * time_table(times, points)
    pol_freq = jnp.einsum("tn,tq->nq", forward, by_momentum, precision=mode)
    momenta = lax.axis_index("tau") * block + jnp.arange(block, dtype=jnp.int32)
    bare = bare_potential(momenta % L, momenta // L, onsite_coupling[0], neighbour_strength[0])
    screened = screen(pol_freq, bare[None, :])
    weight = jnp.where(jnp.arange(NF) == 0, 1.0, 2.0).astype(jnp.float32)
    inverse = time_table(jnp.arange(points, dtype=jnp.int32), points) * weight
    w_columns = jnp.einsum("tn,nq->tq", inverse, screened, precision=mode)

    back = lax.all_to_all(w_columns, "tau", split_axis=0, concat_axis=1, tiled=True)
    back = back[:, :width].reshape(slab, kept, L)
    back_cos = jnp.einsum("flk,kx->flx", back, cos_table(waves, waves, L) / L, precision=mode)
    back_sin = jnp.einsum("flk,kx->flx", back, sin_table(waves, waves, L) / L, precision=mode)
    w_time = jnp.einsum("flx,yl->fxy", back_cos, cos_table(waves, halves, L) * twice, precision=mode) - jnp.einsum(
        "flx,yl->fxy", back_sin, sin_table(waves, halves, L) * twice, precision=mode
    )
    return -propagator * w_time.reshape(slab, sites)


LANES = 128
PAIR = 2 * L
HALF_L = L // 2
KEPT = HALF_L + 1
ROWS_X = 104
Z_ROWS = 216
bf16 = jnp.bfloat16
f32 = jnp.float32
NN = (((1,), (0,)), ((), ()))
NT = (((1,), (1,)), ((), ()))


def halves_of(x):
    high = x.astype(bf16)
    return high, (x - high.astype(f32)).astype(bf16)


def product(a, b, dims):
    return lax.dot_general(a, b, dims, preferred_element_type=f32)


def product3(a, b, dims):
    return product(a[0], b[0], dims) + product(a[0], b[1], dims) + product(a[1], b[0], dims)


def table_halves(table):
    high = np.asarray(table, np.float32).astype(bf16)
    low = (np.asarray(table, np.float64) - high.astype(np.float64)).astype(np.float32).astype(bf16)
    return jnp.asarray(high), jnp.asarray(low)


def np_angle(a, b):
    return 2.0 * np.pi * ((a[:, None] * b[None, :]) % L) / L


def np_twice(a):
    return np.where((a == 0) | (a == HALF_L), 1.0, np.where(a > HALF_L, 0.0, 2.0))


def along_y_table():
    table = np.zeros((256, 512))
    angle = np_angle(np.arange(KEPT), np.arange(L))
    for i, part in enumerate((np.cos(angle), np.sin(angle))):
        table[128 * i : 128 * i + KEPT, 0:L] = part / L
        table[128 * i : 128 * i + KEPT, 256 + 64 : 512] = part / L
    return table_halves(table)


def along_x_table(pairs):
    table = np.zeros((L, 2 * pairs))
    for parity in (0, 1):
        x = 2 * np.arange(pairs) + parity
        angle = np_angle(np.arange(HALF_L), x)
        rows = slice(HALF_L * parity, HALF_L * (parity + 1))
        table[rows, :pairs] = np.cos(angle) * np_twice(x)
        table[rows, pairs:] = -np.sin(angle) * np_twice(x)
    return table_halves(table)


def back_x_table():
    table = np.zeros((2 * ROWS_X, L))
    angle = np_angle(np.arange(KEPT), np.arange(L))
    table[:KEPT] = np.cos(angle) / L
    table[ROWS_X : ROWS_X + KEPT] = np.sin(angle) / L
    return table_halves(table)


def back_y_table():
    table = np.zeros((4, 2 * ROWS_X, 256))
    ky = np.arange(KEPT)
    angle = np_angle(ky, np.arange(L))
    weight = np_twice(ky)[:, None]
    for side in (0, 1):
        for parity in (0, 1):
            columns = slice(64 * parity, 64 * parity + L)
            table[2 * side + parity, :KEPT, columns] = weight * np.cos(angle)
            table[2 * side + parity, ROWS_X : ROWS_X + KEPT, columns] = (
                (2 * side - 1) * weight * np.sin(angle)
            )
    return table_halves(table)


def lane_swap(x):
    return pltpu.roll(x, LANES // 2, 1)


GROUP = 8


def bubble_kernel(limit, own_ref, mirror_ref, flip_ref, high_ref, low_ref, out_ref):
    start = pl.program_id(0) * GROUP
    table = (high_ref[...], low_ref[...])
    flip = flip_ref[...]
    empty = jnp.zeros((64, 256), f32)
    for u in range(GROUP // 2):
        lanes = slice(2 * u * PAIR, (2 * u + 2) * PAIR)
        high, low = halves_of(mirror_ref[:, lanes])
        mirrored = product(flip, high, NN) + product(flip, low, NN)
        bubble = -own_ref[:, lanes] * mirrored
        rows = []
        for v in range(2):
            field = bubble[:, v * PAIR : (v + 1) * PAIR]
            field = jnp.where(start + 2 * u + v < limit, field, 0.0)
            rows.append(jnp.concatenate([field[:, :256], empty], axis=1))
            rows.append(jnp.concatenate([empty, field[:, 128:]], axis=1))
        stacked = jnp.concatenate(rows, axis=0)
        result = product3(table, halves_of(stacked), NT)
        out_ref[2 * u] = result[:, :LANES]
        out_ref[2 * u + 1] = result[:, LANES:]


def bubble_along_y(propagator, mirror, first, pairs):
    half = propagator.shape[0] // 2
    steps = -(-pairs // GROUP)
    shift = first // GROUP
    width = GROUP * PAIR
    high, low = along_y_table()
    flip = jnp.asarray(np.eye(half)[::-1].astype(bf16))
    whole = lambda a: pl.BlockSpec(a.shape, lambda i: (0,) * a.ndim)
    return pl.pallas_call(
        lambda *refs: bubble_kernel(pairs, *refs),
        grid=(steps,),
        in_specs=[
            pl.BlockSpec((half, width), lambda i: (0, i + shift)),
            pl.BlockSpec((half, width), lambda i: (0, i)),
            whole(flip),
            whole(high),
            whole(low),
        ],
        out_specs=pl.BlockSpec((GROUP, 256, LANES), lambda i: (i, 0, 0)),
        out_shape=jax.ShapeDtypeStruct((steps * GROUP, 256, LANES), f32),
        cost_estimate=pl.CostEstimate(
            flops=6 * pairs * 256 * 256 * 256, bytes_accessed=3 * half * pairs * PAIR * 4, transcendentals=0
        ),
        interpret=INTERPRET,
        name="bubble_along_y",
    )(propagator, mirror, flip, high, low)


KY_STEP = 14


def along_x_kernel(counts, *refs):
    parts, (high_ref, low_ref, out_ref) = refs[: len(counts)], refs[len(counts) :]
    table = (high_ref[...], low_ref[...])
    first_half = lax.broadcasted_iota(jnp.int32, (HALF_L, LANES), 1) < LANES // 2

    def lines(ky):
        return jnp.concatenate(
            [
                part[pl.ds(offset + ky, count, stride=256), :]
                for offset in (0, 128)
                for part, count in zip(parts, counts)
            ],
            axis=0,
        )

    first = pl.program_id(0) * KY_STEP

    def body(m, carry):
        ky = first + 2 * m
        both = jnp.concatenate([lines(ky), lines(ky + 1)], axis=1)
        result = product3(table, halves_of(both), NN)
        for v in range(2):
            even = result[:HALF_L, LANES * v : LANES * (v + 1)]
            odd = result[HALF_L:, LANES * v : LANES * (v + 1)]
            out_ref[pl.ds((2 * m + v) * HALF_L, HALF_L), :] = jnp.where(
                first_half, even + lane_swap(odd), lane_swap(even) - odd
            )
        return carry

    lax.fori_loop(0, KY_STEP // 2, body, 0)


def along_x(parts, rows):
    counts = tuple(p.shape[0] for p in parts)
    high, low = along_x_table(sum(counts))
    flat = [p.reshape(-1, LANES) for p in parts]
    whole = lambda a: pl.BlockSpec(a.shape, lambda i: (0,) * a.ndim)
    block = KY_STEP * HALF_L
    return pl.pallas_call(
        lambda *refs: along_x_kernel(counts, *refs),
        grid=(-(-rows // block),),
        in_specs=[whole(a) for a in (*flat, high, low)],
        out_specs=pl.BlockSpec((block, LANES), lambda i: (i, 0)),
        out_shape=jax.ShapeDtypeStruct((rows, LANES), f32),
        cost_estimate=pl.CostEstimate(
            flops=6 * KEPT * L * 256 * LANES, bytes_accessed=12 * 1024 * 1024, transcendentals=0
        ),
        interpret=INTERPRET,
        name="along_x",
    )(*flat, high, low)


def frequency_kernel(side, x_ref, bare_ref, high_ref, low_ref, out_ref):
    sources = x_ref.shape[0]
    first_half = lax.broadcasted_iota(jnp.int32, x_ref.shape[1:], 1) < LANES // 2
    pieces = []
    for k in range(sources // 2):
        near, far = x_ref[k], x_ref[sources - 1 - k]
        if side == 0:
            pieces.append(jnp.where(first_half, near, lane_swap(far)))
        else:
            pieces.append(jnp.where(first_half, lane_swap(near), far))
    table = (high_ref[...], low_ref[...])
    pol = product3(halves_of(jnp.concatenate(pieces, axis=1)), table, NN)
    bare = bare_ref[...]
    screened = bare * bare * pol / jnp.maximum(1.0 - bare * pol, 1.0)
    zero = lax.broadcasted_iota(jnp.int32, screened.shape, 1) == 0
    screened = jnp.where(zero, 0.5 * screened, screened)
    w = product3(halves_of(screened), table, NT)
    for k in range(sources // 2):
        piece = w[:, LANES * k : LANES * (k + 1)]
        out_ref[k] = piece
        out_ref[sources - 1 - k] = piece


ROW_BLOCK = 200


def through_frequencies(x, bare, table, side):
    sources, rows, _ = x.shape
    high, low = table
    whole = lambda a: pl.BlockSpec(a.shape, lambda i: (0,) * a.ndim)
    return pl.pallas_call(
        lambda *refs: frequency_kernel(side, *refs),
        grid=(-(-rows // ROW_BLOCK),),
        in_specs=[
            pl.BlockSpec((sources, ROW_BLOCK, LANES), lambda i: (0, i, 0)),
            pl.BlockSpec((ROW_BLOCK, 1), lambda i: (i, 0)),
            whole(high),
            whole(low),
        ],
        out_specs=pl.BlockSpec((sources, ROW_BLOCK, LANES), lambda i: (0, i, 0)),
        out_shape=jax.ShapeDtypeStruct((sources, rows, LANES), f32),
        cost_estimate=pl.CostEstimate(
            flops=12 * rows * high.shape[0] * high.shape[1],
            bytes_accessed=2 * x.size * 4,
            transcendentals=0,
        ),
        interpret=INTERPRET,
        name="through_frequencies",
    )(x, bare, high, low)


X_STEP = 8


def inverse_kernel(low_ref, high_ref, xh_ref, xl_ref, perm_ref, yh_ref, yl_ref, own_ref, out_ref, z_ref):
    @pl.when(pl.program_id(0) == 0)
    def _():
        z_ref[...] = jnp.zeros_like(z_ref)
        table = (xh_ref[...], xl_ref[...])

        def lines(ky):
            rows = pl.ds(ky * HALF_L, HALF_L)
            return jnp.concatenate([low_ref[rows, :], high_ref[rows, :]], axis=0)

        def put(ky, result):
            z_ref[pl.ds(ky, KEPT, stride=Z_ROWS), :] = result[:KEPT]
            z_ref[pl.ds(ROWS_X + ky, KEPT, stride=Z_ROWS), :] = result[ROWS_X : ROWS_X + KEPT]

        def body(m, carry):
            both = jnp.concatenate([lines(2 * m), lines(2 * m + 1)], axis=1)
            result = product3(table, halves_of(both), NN)
            put(2 * m, result[:, :LANES])
            put(2 * m + 1, result[:, LANES:])
            return carry

        lax.fori_loop(0, KEPT // 2, body, 0)
        put(KEPT - 1, product3(table, halves_of(lines(KEPT - 1)), NN))

    perm = perm_ref[...]
    first = pl.program_id(0) * X_STEP
    for u in range(X_STEP // 2):
        sides = []
        for parity in range(2):
            x = first + 2 * u + parity
            mirror = jnp.where(x > HALF_L, L - x, x)
            case = jnp.where(x > HALF_L, 2, 0) + parity
            lines = halves_of(z_ref[pl.ds(mirror * Z_ROWS, 2 * ROWS_X), :])
            turned = tuple(product(perm, part, NT).astype(bf16) for part in lines)
            sides.append(product3(turned, (yh_ref[case], yl_ref[case]), NN))
        even, odd = sides
        base = u * PAIR
        for start, w in ((0, even[:, :128]), (128, even[:, 128:] + odd[:, :128]), (256, odd[:, 128:])):
            lanes = slice(base + start, base + start + 128)
            out_ref[:, lanes] = -own_ref[:, lanes] * w


def back_to_sites(propagator, lower, upper, perm):
    slab, sites = propagator.shape
    xh, xl = back_x_table()
    yh, yl = back_y_table()
    width = X_STEP * L
    whole = lambda a: pl.BlockSpec(a.shape, lambda i: (0,) * a.ndim)
    moving = pl.BlockSpec((slab, width), lambda i: (0, i))
    return pl.pallas_call(
        inverse_kernel,
        grid=(sites // width,),
        in_specs=[whole(a) for a in (lower, upper, xh, xl, perm, yh, yl)] + [moving],
        out_specs=moving,
        out_shape=jax.ShapeDtypeStruct((slab, sites), f32),
        scratch_shapes=[pltpu.VMEM((KEPT * Z_ROWS, LANES), f32)],
        cost_estimate=pl.CostEstimate(
            flops=10 * L * 128 * 256 * 256, bytes_accessed=2 * propagator.size * 4, transcendentals=0
        ),
        interpret=INTERPRET,
        name="back_to_sites",
    )(lower, upper, xh, xl, perm, yh, yl, propagator)


INTERPRET = False
CUTS = (0, 24, KEPT // 2 + 1)


def with_kernels(propagator, onsite_coupling, neighbour_strength):
    devices = lax.axis_size("tau")
    me = lax.axis_index("tau")
    slab, sites = propagator.shape
    half = slab // 2
    points = slab * devices
    rows = -(-KEPT * HALF_L // (8 * devices)) * 8

    partner = [(d, devices - 1 - d) for d in range(devices)]
    parts = []
    for first, last in zip(CUTS[:-1], CUTS[1:]):
        mirror = lax.ppermute(propagator[half:, first * PAIR : last * PAIR], "tau", partner)
        parts.append(bubble_along_y(propagator, mirror, first, last - first))

    slot = lax.optimization_barrier(jnp.arange(points // 2, dtype=jnp.int32))
    lane = slot % slab
    times = slot - lane + jnp.where(lane < half, lane, slab + half - 1 - lane)
    table = 2.0 * time_table(times, points)
    table_high = lax.reduce_precision(table, 8, 7)
    table = (table_high.astype(bf16), (table - table_high).astype(bf16))

    row = me * rows + jnp.arange(rows, dtype=jnp.int32)
    bare = [
        bare_potential(
            (row % HALF_L + HALF_L * side)[:, None], (row // HALF_L)[:, None], onsite_coupling[0], neighbour_strength[0]
        )
        for side in (0, 1)
    ]
    own_row = jnp.arange(slab, dtype=jnp.int32)
    forth = jnp.where(own_row < half, own_row, slab + half - 1 - own_row)
    back = jnp.where(own_row < half, half + own_row, slab - 1 - own_row)
    source = jnp.where(me < devices // 2, forth, back)
    perm = (source[:, None] == own_row[None, :]).astype(bf16)

    pol_mom = along_x(parts, rows * devices).reshape(devices, rows, LANES)
    by_momentum = lax.all_to_all(pol_mom, "tau", split_axis=0, concat_axis=0, tiled=True)
    returned = []
    for side in (0, 1):
        w = through_frequencies(by_momentum, bare[side], table, side)
        w = lax.all_to_all(w, "tau", split_axis=0, concat_axis=0, tiled=True)
        returned.append(w.reshape(devices * rows, LANES))
    return back_to_sites(propagator, returned[0], returned[1], perm)


def per_device(propagator, onsite_coupling, neighbour_strength):
    fits = propagator.shape[0] == LANES and propagator.shape[1] == L * L
    run = with_kernels if fits else plain
    return run(propagator, onsite_coupling, neighbour_strength)


def solution(mesh):
    in_specs = (P(("grp", "tau"), None), P("grp"), P("grp"))
    out_specs = P(("grp", "tau"), None)
    return jax.shard_map(
        per_device, mesh=mesh, in_specs=in_specs, out_specs=out_specs, check_vma=False
    )
```

```python
import math

import jax
import jax.numpy as jnp
import numpy as np
from jax import lax
from jax.experimental import pallas as pl
from jax.experimental.pallas import tpu as pltpu
from jax.sharding import PartitionSpec as P


L = 192
NF = 1024

mode = lax.Precision.HIGH


def cos_table(rows, columns, period):
    phase = rows[:, None] * columns[None, :] % period
    return jnp.cos(2.0 * jnp.pi * phase.astype(jnp.float32) / period)


def sin_table(rows, columns, period):
    phase = rows[:, None] * columns[None, :] % period
    return jnp.sin(2.0 * jnp.pi * phase.astype(jnp.float32) / period)


def time_table(times, points):
    frequency = jnp.arange(NF, dtype=jnp.int32)[None, :]
    phase = frequency * (2 * times[:, None] + 1) % (2 * points)
    return jnp.cos(jnp.pi * phase.astype(jnp.float32) / points) / math.sqrt(points)


def bare_potential(first, second, onsite, nearest):
    first = first.astype(jnp.float32)
    second = second.astype(jnp.float32)
    return onsite + 2.0 * nearest * (
        jnp.cos(2.0 * jnp.pi * first / L) + jnp.cos(2.0 * jnp.pi * second / L)
    )


def screen(pol_mom, bare):
    denom = jnp.maximum(1.0 - bare * pol_mom, 1.0)
    return bare * bare * pol_mom / denom


def plain(propagator, onsite_coupling, neighbour_strength):
    devices = lax.axis_size("tau")
    slab, sites = propagator.shape
    half = slab // 2
    points = slab * devices
    kept = L // 2 + 1
    width = kept * L
    block = -(-width // (8 * devices)) * 8
    padded = block * devices

    waves = jnp.arange(L, dtype=jnp.int32)
    halves = jnp.arange(kept, dtype=jnp.int32)
    twice = jnp.where((halves == 0) | (halves == L // 2), 1.0, 2.0).astype(jnp.float32)

    partner = [(d, devices - 1 - d) for d in range(devices)]
    mirrored = lax.ppermute(propagator[half:, :width], "tau", partner)
    polarization = -propagator[:half, :width] * mirrored[::-1]

    field = polarization.reshape(half, kept, L)
    along_cos = cos_table(halves, waves, L) / L
    along_sin = sin_table(halves, waves, L) / L
    first_cos = jnp.einsum("fxy,ly->fxl", field, along_cos, precision=mode)
    first_sin = jnp.einsum("fxy,ly->fxl", field, along_sin, precision=mode)
    cos_x = cos_table(waves, halves, L)
    sin_x = sin_table(waves, halves, L)
    pol_mom = jnp.einsum("fxl,kx->flk", first_cos, cos_x * twice, precision=mode) - jnp.einsum(
        "fxl,kx->flk", first_sin, sin_x * twice, precision=mode
    )
    pol_mom = jnp.pad(pol_mom.reshape(half, width), ((0, 0), (0, padded - width)))
    by_momentum = lax.all_to_all(pol_mom, "tau", split_axis=1, concat_axis=0, tiled=True)

    held = jnp.arange(devices * half, dtype=jnp.int32)
    times = held // half * slab + held % half
    forward = 2.0 * time_table(times, points)
    pol_freq = jnp.einsum("tn,tq->nq", forward, by_momentum, precision=mode)
    momenta = lax.axis_index("tau") * block + jnp.arange(block, dtype=jnp.int32)
    bare = bare_potential(momenta % L, momenta // L, onsite_coupling[0], neighbour_strength[0])
    screened = screen(pol_freq, bare[None, :])
    weight = jnp.where(jnp.arange(NF) == 0, 1.0, 2.0).astype(jnp.float32)
    inverse = time_table(jnp.arange(points, dtype=jnp.int32), points) * weight
    w_columns = jnp.einsum("tn,nq->tq", inverse, screened, precision=mode)

    back = lax.all_to_all(w_columns, "tau", split_axis=0, concat_axis=1, tiled=True)
    back = back[:, :width].reshape(slab, kept, L)
    back_cos = jnp.einsum("flk,kx->flx", back, cos_table(waves, waves, L) / L, precision=mode)
    back_sin = jnp.einsum("flk,kx->flx", back, sin_table(waves, waves, L) / L, precision=mode)
    w_time = jnp.einsum("flx,yl->fxy", back_cos, cos_table(waves, halves, L) * twice, precision=mode) - jnp.einsum(
        "flx,yl->fxy", back_sin, sin_table(waves, halves, L) * twice, precision=mode
    )
    return -propagator * w_time.reshape(slab, sites)


LANES = 128
PAIR = 2 * L
HALF_L = L // 2
KEPT = HALF_L + 1
ROWS_X = 104
INTERPRET = False
MIB = 1024 * 1024
bf16 = jnp.bfloat16
f32 = jnp.float32
NN = (((1,), (0,)), ((), ()))
NT = (((1,), (1,)), ((), ()))


def halves_of(x):
    high = x.astype(bf16)
    return high, (x - high.astype(f32)).astype(bf16)


def product(a, b, dims):
    return lax.dot_general(a, b, dims, preferred_element_type=f32)


def product3(a, b, dims):
    return product(a[0], b[0], dims) + product(a[0], b[1], dims) + product(a[1], b[0], dims)


def table_halves(table):
    high = np.asarray(table, np.float32).astype(bf16)
    low = (np.asarray(table, np.float64) - high.astype(np.float64)).astype(np.float32).astype(bf16)
    return jnp.asarray(high), jnp.asarray(low)


def np_angle(a, b):
    return 2.0 * np.pi * ((a[:, None] * b[None, :]) % L) / L


def np_twice(a):
    return np.where((a == 0) | (a == HALF_L), 1.0, np.where(a > HALF_L, 0.0, 2.0))


def along_y_table():
    table = np.zeros((256, 512))
    angle = np_angle(np.arange(KEPT), np.arange(L))
    for i, part in enumerate((np.cos(angle), np.sin(angle))):
        table[128 * i : 128 * i + KEPT, 0:L] = part / L
        table[128 * i : 128 * i + KEPT, 256 + 64 : 512] = part / L
    return table_halves(table)


def along_x_table(pairs):
    table = np.zeros((L, 2 * pairs))
    for parity in (0, 1):
        x = 2 * np.arange(pairs) + parity
        angle = np_angle(np.arange(HALF_L), x)
        rows = slice(HALF_L * parity, HALF_L * (parity + 1))
        table[rows, :pairs] = np.cos(angle) * np_twice(x)
        table[rows, pairs:] = -np.sin(angle) * np_twice(x)
    return table_halves(table)


anywhere = pl.BlockSpec(memory_space=pl.ANY)


def lane_swap(x):
    return pltpu.roll(x, LANES // 2, 1)


GROUP = 8


def bubble_kernel(limit, own_ref, mirror_ref, flip_ref, high_ref, low_ref, out_ref):
    start = pl.program_id(0) * GROUP
    table = (high_ref[...], low_ref[...])
    flip = flip_ref[...]
    first_half = lax.broadcasted_iota(jnp.int32, (256, LANES), 1) < LANES // 2
    for u in range(0, GROUP, 4):
        lines = []
        for v in range(u, u + 4, 2):
            lanes = slice(v * PAIR, (v + 2) * PAIR)
            high, low = halves_of(mirror_ref[:, lanes])
            mirrored = product(flip, high, NN) + product(flip, low, NN)
            field = -own_ref[:, lanes] * mirrored
            lines += [field[:, :PAIR], field[:, PAIR:]]
        lines = [jnp.where(start + u + i < limit, line, 0.0) for i, line in enumerate(lines)]
        even = jnp.concatenate([line[:, :256] for line in lines], axis=0)
        odd = jnp.concatenate([line[:, 128:] for line in lines], axis=0)
        even = product3((table[0][:, :256], table[1][:, :256]), halves_of(even), NT)
        odd = product3((table[0][:, 256:], table[1][:, 256:]), halves_of(odd), NT)
        for v in range(2):
            lanes = slice(v * LANES, (v + 1) * LANES)
            near, far = even[:, lanes], odd[:, lanes]
            out_ref[u + 2 * v] = jnp.where(first_half, near, lane_swap(far))
            out_ref[u + 2 * v + 1] = jnp.where(first_half, lane_swap(near), far)


def bubble_along_y(propagator, mirror, first, pairs, before, after):
    half = propagator.shape[0] // 2
    steps = -(-pairs // GROUP)
    shift = first // GROUP
    width = GROUP * PAIR
    high, low = along_y_table()
    flip = jnp.asarray(np.eye(half)[::-1].astype(bf16))
    whole = lambda a: pl.BlockSpec(a.shape, lambda i: (0,) * a.ndim)
    total = -(-(KEPT // 2 + 1) // GROUP) * GROUP
    earlier = [] if before is None else [before]
    return pl.pallas_call(
        lambda *refs: bubble_kernel(pairs, *refs[:5], refs[-1]),
        grid=(steps,),
        in_specs=[
            pl.BlockSpec((half, width), lambda i: (0, i + shift)),
            pl.BlockSpec((half, width), lambda i: (0, i)),
            whole(flip),
            whole(high),
            whole(low),
        ]
        + [anywhere] * (len(earlier) + len(after)),
        out_specs=pl.BlockSpec((GROUP, 256, LANES), lambda i: (i + shift, 0, 0)),
        out_shape=jax.ShapeDtypeStruct((total, 256, LANES), f32),
        input_output_aliases={5: 0} if earlier else {},
        cost_estimate=pl.CostEstimate(
            flops=6 * pairs * 256 * 256 * 256, bytes_accessed=3 * half * pairs * PAIR * 4, transcendentals=0
        ),
        compiler_params=pltpu.CompilerParams(vmem_limit_bytes=16 * MIB),
        interpret=INTERPRET,
        name="bubble_along_y",
    )(propagator, mirror, flip, high, low, *earlier, *after)


def whole(array):
    return pl.BlockSpec(array.shape, lambda *i: (0,) * array.ndim, pipeline_mode=pl.Buffered(1))


def along_x_kernel(first, span, copies, counts, *refs):
    parts, (high_ref, low_ref), out_ref = refs[: len(counts)], refs[len(counts) : len(counts) + 2], refs[-1]
    table = (high_ref[...], low_ref[...])
    first_half = lax.broadcasted_iota(jnp.int32, (HALF_L, LANES), 1) < LANES // 2
    start = first + pl.program_id(0) * span

    def lines(ky):
        return jnp.concatenate(
            [
                part[pl.ds(offset + ky, count, stride=256), :]
                for offset in (0, 128)
                for part, count in zip(parts, counts)
            ],
            axis=0,
        )

    for m in range(0, span, 2):
        both = jnp.concatenate([lines(start + m), lines(start + m + 1)], axis=1)
        result = product3(table, halves_of(both), NN)
        for v in range(2):
            even = result[:HALF_L, LANES * v : LANES * (v + 1)]
            odd = result[HALF_L:, LANES * v : LANES * (v + 1)]
            both_halves = jnp.where(first_half, even + lane_swap(odd), lane_swap(even) - odd)
            for copy in range(copies):
                out_ref[copy, (m + v) * HALF_L : (m + v + 1) * HALF_L, :] = both_halves


def along_x(parts, first, span, rows, copies, after):
    counts = tuple(p.shape[0] for p in parts)
    high, low = along_x_table(sum(counts))
    flat = [p.reshape(-1, LANES) for p in parts]
    block = span * HALF_L
    return pl.pallas_call(
        lambda *refs: along_x_kernel(first, span, copies, counts, *refs),
        grid=(-(-rows // block),),
        in_specs=[whole(a) for a in (*flat, high, low)] + [anywhere] * len(after),
        out_specs=pl.BlockSpec((copies, block, LANES), lambda i: (0, i, 0)),
        out_shape=jax.ShapeDtypeStruct((copies, rows, LANES), f32),
        cost_estimate=pl.CostEstimate(
            flops=6 * rows * 2 * 256 * LANES, bytes_accessed=12 * 1024 * 1024, transcendentals=0
        ),
        compiler_params=pltpu.CompilerParams(vmem_limit_bytes=20 * MIB),
        interpret=INTERPRET,
        name="along_x",
    )(*flat, high, low, *after)


def gathered(x, lane):
    return jnp.take_along_axis(x, lane, axis=1, mode="promise_in_bounds")


def frequency_kernel(both_sides, sign_ref, x_ref, bare_ref, *refs):
    tables, out_ref = refs[:8], refs[-1]
    forth = ((tables[0][...], tables[1][...]), (tables[2][...], tables[3][...]))
    back = ((tables[4][...], tables[5][...]), (tables[6][...], tables[7][...]))
    hs = x_ref.shape[0] // 2
    tile = x_ref.shape[1:]
    lane = lax.broadcasted_iota(jnp.int32, tile, 1)
    first_half = lane < LANES // 2
    mixed = [
        [x_ref[k] + x_ref[k + hs] for k in range(hs)],
        [x_ref[k] - x_ref[k + hs] for k in range(hs)],
    ]
    for side in range(2):
        bare = bare_ref[side]
        result = []
        for parity in range(2):
            u = mixed[parity]
            pieces = []
            for k in range(0, hs, 2):
                if side == 0:
                    pieces.append(jnp.where(first_half, u[k], lane_swap(u[k + 1])))
                else:
                    pieces.append(jnp.where(first_half, lane_swap(u[k]), u[k + 1]))
            pol = product3(halves_of(jnp.concatenate(pieces, axis=1)), forth[parity], NN)
            screened = bare * bare * pol / jnp.maximum(1.0 - bare * pol, 1.0)
            if parity == 0:
                zero = lax.broadcasted_iota(jnp.int32, screened.shape, 1) == 0
                screened = jnp.where(zero, 0.5 * screened, screened)
            result.append(product3(halves_of(screened), back[parity], NN))
        for d in range(hs // 2):
            lanes = slice(LANES * d, LANES * (d + 1))
            even, odd = result[0][:, lanes], result[1][:, lanes]
            if not both_sides:
                odd = odd * sign_ref[0]
            near, far = even + odd, even - odd
            out_ref[d, side] = near
            out_ref[hs - 1 - d, side] = gathered(far, LANES - 1 - lane)
            if both_sides:
                out_ref[hs + d, side] = far
                out_ref[2 * hs - 1 - d, side] = gathered(near, LANES - 1 - lane)


def through_frequencies(x, bare, tables, block, sign, both_sides, after):
    sources, rows, _ = x.shape
    slabs = sources if both_sides else sources // 2
    return pl.pallas_call(
        lambda *refs: frequency_kernel(both_sides, *refs),
        grid=(-(-rows // block),),
        in_specs=[
            pl.BlockSpec(memory_space=pltpu.SMEM),
            pl.BlockSpec((sources, block, LANES), lambda i: (0, i, 0)),
            pl.BlockSpec((2, block, 1), lambda i: (0, i, 0)),
        ]
        + [whole(a) for a in tables]
        + [anywhere] * len(after),
        out_specs=pl.BlockSpec((slabs, 2, block, LANES), lambda i: (0, 0, i, 0)),
        out_shape=jax.ShapeDtypeStruct((slabs, 2, rows, LANES), f32),
        cost_estimate=pl.CostEstimate(
            flops=48 * rows * 512 * 512, bytes_accessed=3 * x.size * 4, transcendentals=0
        ),
        interpret=INTERPRET,
        name="through_frequencies",
    )(sign, x, bare, *tables, *after)


def line_order():
    return np.concatenate([np.arange(1, KEPT), [0]])


def back_x_table():
    table = np.zeros((2 * ROWS_X, L))
    angle = np_angle(line_order(), np.arange(L))
    table[:KEPT] = np.cos(angle) / L
    table[ROWS_X : ROWS_X + KEPT] = np.sin(angle) / L
    return table_halves(table)


def back_x_kernel(count, depth, sines, *refs):
    lower_ref, upper_ref, high_ref, low_ref, z_ref = refs
    flat = [r.reshape(r.shape[0] * r.shape[1], LANES) for r in (lower_ref, upper_ref)]
    back_x(count, depth, sines, flat, high_ref, low_ref, z_ref)


def gather_back_x_kernel(count, depth, sines, own_ref, *refs):
    blocks, (high_ref, low_ref, z_ref, flat_ref) = refs[:-4], refs[-4:]
    rows = blocks[0].shape[1]
    for k, block in enumerate(blocks):
        place = pl.ds(pl.multiple_of((own_ref[0] ^ k) * rows, 8), rows)
        for side in range(2):
            flat_ref[side, place, :] = block[side]
    back_x(count, depth, sines, [flat_ref.at[0], flat_ref.at[1]], high_ref, low_ref, z_ref)


def back_x(count, depth, sines, flat, high_ref, low_ref, z_ref):
    table = (high_ref[...], low_ref[...])
    z_ref[...] = jnp.zeros_like(z_ref)

    def lines(ky):
        rows = pl.ds(ky * HALF_L, HALF_L)
        return jnp.concatenate([flat[0][rows, :], flat[1][rows, :]], axis=0)

    def put(ky, result):
        z_ref[pl.ds(ky, KEPT, stride=depth), :] = result[:KEPT]
        z_ref[pl.ds(sines + ky, KEPT, stride=depth), :] = result[ROWS_X : ROWS_X + KEPT]

    def pair(ky):
        both = jnp.concatenate([lines(ky), lines(ky + 1)], axis=1)
        result = product3(table, halves_of(both), NN)
        put(ky, result[:, :LANES])
        put(ky + 1, result[:, LANES:])

    unrolled = 4

    def body(m, carry):
        for v in range(unrolled):
            pair(2 * (unrolled * m + v))
        return carry

    lax.fori_loop(0, count // (2 * unrolled), body, 0)
    for ky in range(count // (2 * unrolled) * 2 * unrolled, count - 1, 2):
        pair(ky)
    if count % 2:
        put(count - 1, product3(table, halves_of(lines(count - 1)), NN))


def back_x_depth(count):
    sines = -(-count // 8) * 8
    return sines, (2 * sines // 8 | 1) * 8


def back_along_x(w, count):
    sources, _, rows, _ = w.shape
    high, low = back_x_table()
    sines, depth = back_x_depth(count)
    side = lambda s: pl.BlockSpec(
        (sources, None, rows, LANES), lambda i: (0, s, 0, 0), pipeline_mode=pl.Buffered(1)
    )
    return pl.pallas_call(
        lambda *refs: back_x_kernel(count, depth, sines, *refs),
        grid=(1,),
        in_specs=[side(0), side(1), whole(high), whole(low)],
        out_specs=pl.BlockSpec((KEPT * depth, LANES), lambda i: (0, 0)),
        out_shape=jax.ShapeDtypeStruct((KEPT * depth, LANES), f32),
        cost_estimate=pl.CostEstimate(
            flops=6 * count * 256 * 256 * LANES, bytes_accessed=10 * 1024 * 1024, transcendentals=0
        ),
        compiler_params=pltpu.CompilerParams(vmem_limit_bytes=24 * MIB),
        interpret=INTERPRET,
        name="back_along_x",
    )(w, w, high, low)


def gather_back_along_x(blocks, own, count):
    _, rows, _ = blocks[0].shape
    high, low = back_x_table()
    sines, depth = back_x_depth(count)
    return pl.pallas_call(
        lambda *refs: gather_back_x_kernel(count, depth, sines, *refs),
        grid=(1,),
        in_specs=[pl.BlockSpec(memory_space=pltpu.SMEM)] + [whole(a) for a in (*blocks, high, low)],
        out_specs=pl.BlockSpec((KEPT * depth, LANES), lambda i: (0, 0)),
        out_shape=jax.ShapeDtypeStruct((KEPT * depth, LANES), f32),
        scratch_shapes=[pltpu.VMEM((2, len(blocks) * rows, LANES), f32)],
        cost_estimate=pl.CostEstimate(
            flops=6 * count * 256 * 256 * LANES, bytes_accessed=10 * 1024 * 1024, transcendentals=0
        ),
        compiler_params=pltpu.CompilerParams(vmem_limit_bytes=24 * MIB),
        interpret=INTERPRET,
        name="gather_back_along_x",
    )(own, *blocks, high, low)


def back_y_table(chunks):
    tables = []
    first = 0
    y = np.arange(LANES)
    for count in chunks:
        sines, depth = back_x_depth(count)
        ky = np.arange(first, first + count)
        angle = np_angle(ky, y)
        table = np.zeros((depth, 2 * LANES))
        table[:count, :LANES] = np_twice(ky)[:, None] * np.cos(angle)
        table[sines : sines + count, LANES:] = np_twice(ky)[:, None] * np.sin(angle)
        tables.append(table)
        first += count
    return table_halves(np.concatenate(tables, axis=0))


X_STEP = 8


def back_y_kernel(depths, *refs):
    n = len(depths)
    blocks, firsts = refs[:n], refs[n : 2 * n]
    high_ref, low_ref, own_ref, out_ref, minus_ref, plus_ref = refs[2 * n :]
    step, side = pl.program_id(0), pl.program_id(1)
    table = (high_ref[...], low_ref[...])
    lane = lax.broadcasted_iota(jnp.int32, (LANES, LANES), 1)
    turned_lane = (LANES // 2 - lane) & (LANES - 1)

    def fill(slot, parts):
        lines = jnp.concatenate(parts, axis=0).T
        result = product3(halves_of(lines), table, NN)
        cosines, sines = result[:, :LANES], result[:, LANES:]
        minus_ref[slot] = cosines - sines
        plus_ref[slot] = cosines + sines

    @pl.when((step == 0) & (side == 0))
    def _():
        fill(0, [r[...] for r in firsts])

    @pl.when(side == 0)
    def _():
        for s in range(X_STEP):
            fill(s + 1, [r[s * d : (s + 1) * d, :] for r, d in zip(blocks, depths)])

    def emit(near_ref, far_ref, slots):
        for u in range(X_STEP // 2):
            even, odd = slots[2 * u], slots[2 * u + 1]
            near = near_ref[even]
            far = gathered(far_ref[even], turned_lane)
            near_odd = lane_swap(near_ref[odd])
            far_odd = lane_swap(gathered(far_ref[odd], turned_lane))
            tiles = (
                jnp.where(lane <= HALF_L, near, far),
                jnp.where(lane < LANES // 2, far, near_odd),
                jnp.where(lane <= HALF_L - LANES // 2, near_odd, far_odd),
            )
            for i, w in enumerate(tiles):
                lanes = slice(u * PAIR + i * LANES, u * PAIR + (i + 1) * LANES)
                out_ref[:, lanes] = -own_ref[:, lanes] * w

    @pl.when(side == 0)
    def _():
        emit(minus_ref, plus_ref, list(range(X_STEP)))

    @pl.when(side == 1)
    def _():
        emit(plus_ref, minus_ref, list(range(X_STEP, 0, -1)))
        minus_ref[0] = minus_ref[X_STEP]
        plus_ref[0] = plus_ref[X_STEP]


def back_along_y(propagator, parts, chunks):
    slab, sites = propagator.shape
    high, low = back_y_table(chunks)
    depths = tuple(back_x_depth(c)[1] for c in chunks)
    width = X_STEP * L
    steps = HALF_L // X_STEP
    moving = pl.BlockSpec((slab, width), lambda i, j: (0, jnp.where(j == 0, i, 2 * steps - 1 - i)))
    return pl.pallas_call(
        lambda *refs: back_y_kernel(depths, *refs),
        grid=(steps, 2),
        in_specs=[pl.BlockSpec((X_STEP * d, LANES), lambda i, j: (i, 0)) for d in depths]
        + [pl.BlockSpec((d, LANES), lambda i, j: (HALF_L, 0)) for d in depths]
        + [whole(high), whole(low), moving],
        out_specs=moving,
        out_shape=jax.ShapeDtypeStruct((slab, sites), f32),
        scratch_shapes=[pltpu.VMEM((X_STEP + 1, LANES, LANES), f32)] * 2,
        cost_estimate=pl.CostEstimate(
            flops=6 * KEPT * 128 * 256 * 256, bytes_accessed=2 * propagator.size * 4, transcendentals=0
        ),
        compiler_params=pltpu.CompilerParams(vmem_limit_bytes=12 * MIB),
        interpret=INTERPRET,
        name="back_along_y",
    )(*parts, *parts, high, low, propagator)


CUTS = (0, 40, KEPT // 2 + 1)
CHUNKS = ((33, 12, 200, True), (32, 8, 96, False), (32, 8, 96, False))


def frequency_tables(points, slab):
    half = slab // 2
    quarter = points // 4
    slot = lax.optimization_barrier(jnp.arange(quarter, dtype=jnp.int32))
    count = lax.optimization_barrier(jnp.arange(NF // 2, dtype=jnp.int32))
    held = slot // half * slab + slot % half
    tables = []
    for times, turned in ((held, False), (slot, True)):
        for parity in (0, 1):
            n = 2 * count + parity
            a, b = (n[:, None], times[None, :]) if turned else (n[None, :], times[:, None])
            phase = a * (2 * b + 1) % (2 * points)
            table = jnp.cos(jnp.pi * phase.astype(f32) / points) * (2.0 / math.sqrt(points))
            high = lax.reduce_precision(table, 8, 7)
            tables += [high.astype(bf16), (table - high).astype(bf16)]
    return tables


def with_kernels(propagator, onsite_coupling, neighbour_strength):
    devices = lax.axis_size("tau")
    me = lax.axis_index("tau")
    slab, _ = propagator.shape
    half = slab // 2

    partner = [(d, devices - 1 - d) for d in range(devices)]
    tables = frequency_tables(slab * devices, slab)
    lines = None
    for first, last in zip(CUTS[:-1], CUTS[1:]):
        mirror = lax.ppermute(propagator[half:, first * PAIR : last * PAIR], "tau", partner)
        lines = bubble_along_y(propagator, mirror, first, last - first, lines, [] if first else tables)

    first = 0
    returned = []
    moved, turned = [], []
    sides = devices // 2
    own = (me % sides)[None].astype(jnp.int32)
    sign = jnp.where(me < sides, 1.0, -1.0)[None].astype(f32)
    for count, span, block, shared in CHUNKS:
        owners = sides if shared else devices
        rows = -(-count * HALF_L // (8 * owners)) * 8
        pol_mom = along_x([lines], first, span, rows * owners, devices // owners, moved)
        moved = [pol_mom]
        pol_mom = pol_mom.reshape(devices, rows, LANES)
        by_momentum = lax.all_to_all(pol_mom, "tau", split_axis=0, concat_axis=0, tiled=True)
        row = me % owners * rows + jnp.arange(rows, dtype=jnp.int32)
        bare = jnp.stack(
            [
                bare_potential(
                    row % HALF_L + HALF_L * side, first + row // HALF_L, onsite_coupling[0], neighbour_strength[0]
                )
                for side in (0, 1)
            ]
        )[:, :, None]
        w = through_frequencies(by_momentum, bare, tables, block, sign, not shared, turned)
        turned = [w]
        if shared:
            blocks = [lax.dynamic_index_in_dim(w, own[0] ^ k, 0, keepdims=False) for k in range(sides)]
            for k in range(1, sides):
                blocks[k] = lax.ppermute(blocks[k], "tau", [(d, d ^ k) for d in range(devices)])
            returned.append(gather_back_along_x(blocks, own, count))
        else:
            w = lax.all_to_all(w, "tau", split_axis=0, concat_axis=0, tiled=True)
            returned.append(back_along_x(w, count))
        first += count
    return back_along_y(propagator, returned, [c[0] for c in CHUNKS])


def per_device(propagator, onsite_coupling, neighbour_strength):
    slab, sites = propagator.shape
    devices = lax.axis_size("tau")
    fits = slab == LANES and sites == L * L and 4 * NF == 2 * slab * devices and devices & (devices - 1) == 0
    run = with_kernels if fits else plain
    return run(propagator, onsite_coupling, neighbour_strength)


def solution(mesh):
    in_specs = (P(("grp", "tau"), None), P("grp"), P("grp"))
    out_specs = P(("grp", "tau"), None)
    return jax.shard_map(
        per_device, mesh=mesh, in_specs=in_specs, out_specs=out_specs, check_vma=False
    )
```

```python
import math

import jax
import jax.numpy as jnp
import numpy as np
from jax import lax
from jax.experimental import pallas as pl
from jax.experimental.pallas import tpu as pltpu
from jax.sharding import PartitionSpec as P


L = 192
NF = 1024

mode = lax.Precision.HIGH


def cos_table(rows, columns, period):
    phase = rows[:, None] * columns[None, :] % period
    return jnp.cos(2.0 * jnp.pi * phase.astype(jnp.float32) / period)


def sin_table(rows, columns, period):
    phase = rows[:, None] * columns[None, :] % period
    return jnp.sin(2.0 * jnp.pi * phase.astype(jnp.float32) / period)


def time_table(times, points):
    frequency = jnp.arange(NF, dtype=jnp.int32)[None, :]
    phase = frequency * (2 * times[:, None] + 1) % (2 * points)
    return jnp.cos(jnp.pi * phase.astype(jnp.float32) / points) / math.sqrt(points)


def bare_potential(first, second, onsite, nearest):
    first = first.astype(jnp.float32)
    second = second.astype(jnp.float32)
    return onsite + 2.0 * nearest * (
        jnp.cos(2.0 * jnp.pi * first / L) + jnp.cos(2.0 * jnp.pi * second / L)
    )


def screen(pol_mom, bare):
    denom = jnp.maximum(1.0 - bare * pol_mom, 1.0)
    return bare * bare * pol_mom / denom


def plain(propagator, onsite_coupling, neighbour_strength):
    devices = lax.axis_size("tau")
    slab, sites = propagator.shape
    half = slab // 2
    points = slab * devices
    kept = L // 2 + 1
    width = kept * L
    block = -(-width // (8 * devices)) * 8
    padded = block * devices

    waves = jnp.arange(L, dtype=jnp.int32)
    halves = jnp.arange(kept, dtype=jnp.int32)
    twice = jnp.where((halves == 0) | (halves == L // 2), 1.0, 2.0).astype(jnp.float32)

    partner = [(d, devices - 1 - d) for d in range(devices)]
    mirrored = lax.ppermute(propagator[half:, :width], "tau", partner)
    polarization = -propagator[:half, :width] * mirrored[::-1]

    field = polarization.reshape(half, kept, L)
    along_cos = cos_table(halves, waves, L) / L
    along_sin = sin_table(halves, waves, L) / L
    first_cos = jnp.einsum("fxy,ly->fxl", field, along_cos, precision=mode)
    first_sin = jnp.einsum("fxy,ly->fxl", field, along_sin, precision=mode)
    cos_x = cos_table(waves, halves, L)
    sin_x = sin_table(waves, halves, L)
    pol_mom = jnp.einsum("fxl,kx->flk", first_cos, cos_x * twice, precision=mode) - jnp.einsum(
        "fxl,kx->flk", first_sin, sin_x * twice, precision=mode
    )
    pol_mom = jnp.pad(pol_mom.reshape(half, width), ((0, 0), (0, padded - width)))
    by_momentum = lax.all_to_all(pol_mom, "tau", split_axis=1, concat_axis=0, tiled=True)

    held = jnp.arange(devices * half, dtype=jnp.int32)
    times = held // half * slab + held % half
    forward = 2.0 * time_table(times, points)
    pol_freq = jnp.einsum("tn,tq->nq", forward, by_momentum, precision=mode)
    momenta = lax.axis_index("tau") * block + jnp.arange(block, dtype=jnp.int32)
    bare = bare_potential(momenta % L, momenta // L, onsite_coupling[0], neighbour_strength[0])
    screened = screen(pol_freq, bare[None, :])
    weight = jnp.where(jnp.arange(NF) == 0, 1.0, 2.0).astype(jnp.float32)
    inverse = time_table(jnp.arange(points, dtype=jnp.int32), points) * weight
    w_columns = jnp.einsum("tn,nq->tq", inverse, screened, precision=mode)

    back = lax.all_to_all(w_columns, "tau", split_axis=0, concat_axis=1, tiled=True)
    back = back[:, :width].reshape(slab, kept, L)
    back_cos = jnp.einsum("flk,kx->flx", back, cos_table(waves, waves, L) / L, precision=mode)
    back_sin = jnp.einsum("flk,kx->flx", back, sin_table(waves, waves, L) / L, precision=mode)
    w_time = jnp.einsum("flx,yl->fxy", back_cos, cos_table(waves, halves, L) * twice, precision=mode) - jnp.einsum(
        "flx,yl->fxy", back_sin, sin_table(waves, halves, L) * twice, precision=mode
    )
    return -propagator * w_time.reshape(slab, sites)


LANES = 128
PAIR = 2 * L
HALF_L = L // 2
KEPT = HALF_L + 1
ROWS_X = 104
INTERPRET = False
MIB = 1024 * 1024
bf16 = jnp.bfloat16
f32 = jnp.float32
NN = (((1,), (0,)), ((), ()))
NT = (((1,), (1,)), ((), ()))


def halves_of(x):
    high = x.astype(bf16)
    return high, (x - high.astype(f32)).astype(bf16)


def product(a, b, dims):
    return lax.dot_general(a, b, dims, preferred_element_type=f32)


def product3(a, b, dims):
    return product(a[0], b[0], dims) + product(a[0], b[1], dims) + product(a[1], b[0], dims)


def table_halves(table):
    high = np.asarray(table, np.float32).astype(bf16)
    low = (np.asarray(table, np.float64) - high.astype(np.float64)).astype(np.float32).astype(bf16)
    return jnp.asarray(high), jnp.asarray(low)


def np_angle(a, b):
    return 2.0 * np.pi * ((a[:, None] * b[None, :]) % L) / L


def np_twice(a):
    return np.where((a == 0) | (a == HALF_L), 1.0, np.where(a > HALF_L, 0.0, 2.0))


def along_y_table():
    table = np.zeros((256, 512))
    angle = np_angle(np.arange(KEPT), np.arange(L))
    for i, part in enumerate((np.cos(angle), np.sin(angle))):
        table[128 * i : 128 * i + KEPT, 0:L] = part / L
        table[128 * i : 128 * i + KEPT, 256 + 64 : 512] = part / L
    return table_halves(table)


def along_x_table(pairs):
    table = np.zeros((L, 2 * pairs))
    for parity in (0, 1):
        x = 2 * np.arange(pairs) + parity
        angle = np_angle(np.arange(HALF_L), x)
        rows = slice(HALF_L * parity, HALF_L * (parity + 1))
        table[rows, :pairs] = np.cos(angle) * np_twice(x)
        table[rows, pairs:] = -np.sin(angle) * np_twice(x)
    return table_halves(table)


anywhere = pl.BlockSpec(memory_space=pl.ANY)


def lane_swap(x):
    return pltpu.roll(x, LANES // 2, 1)


GROUP = 8


def bubble_kernel(limit, own_ref, mirror_ref, flip_ref, high_ref, low_ref, out_ref):
    start = pl.program_id(0) * GROUP
    table = (high_ref[...], low_ref[...])
    flip = flip_ref[...]
    first_half = lax.broadcasted_iota(jnp.int32, (256, LANES), 1) < LANES // 2
    for u in range(0, GROUP, 4):
        lines = []
        for v in range(u, u + 4, 2):
            lanes = slice(v * PAIR, (v + 2) * PAIR)
            high, low = halves_of(mirror_ref[:, lanes])
            mirrored = product(flip, high, NN) + product(flip, low, NN)
            field = -own_ref[:, lanes] * mirrored
            lines += [field[:, :PAIR], field[:, PAIR:]]
        lines = [jnp.where(start + u + i < limit, line, 0.0) for i, line in enumerate(lines)]
        even = jnp.concatenate([line[:, :256] for line in lines], axis=0)
        odd = jnp.concatenate([line[:, 128:] for line in lines], axis=0)
        even = product3((table[0][:, :256], table[1][:, :256]), halves_of(even), NT)
        odd = product3((table[0][:, 256:], table[1][:, 256:]), halves_of(odd), NT)
        for v in range(2):
            lanes = slice(v * LANES, (v + 1) * LANES)
            near, far = even[:, lanes], odd[:, lanes]
            out_ref[u + 2 * v] = jnp.where(first_half, near, lane_swap(far))
            out_ref[u + 2 * v + 1] = jnp.where(first_half, lane_swap(near), far)


def bubble_along_y(propagator, mirror, first, pairs, before, after):
    half = propagator.shape[0] // 2
    steps = -(-pairs // GROUP)
    shift = first // GROUP
    width = GROUP * PAIR
    high, low = along_y_table()
    flip = jnp.asarray(np.eye(half)[::-1].astype(bf16))
    whole = lambda a: pl.BlockSpec(a.shape, lambda i: (0,) * a.ndim)
    total = -(-(KEPT // 2 + 1) // GROUP) * GROUP
    earlier = [] if before is None else [before]
    return pl.pallas_call(
        lambda *refs: bubble_kernel(pairs, *refs[:5], refs[-1]),
        grid=(steps,),
        in_specs=[
            pl.BlockSpec((half, width), lambda i: (0, i + shift)),
            pl.BlockSpec((half, width), lambda i: (0, i)),
            whole(flip),
            whole(high),
            whole(low),
        ]
        + [anywhere] * (len(earlier) + len(after)),
        out_specs=pl.BlockSpec((GROUP, 256, LANES), lambda i: (i + shift, 0, 0)),
        out_shape=jax.ShapeDtypeStruct((total, 256, LANES), f32),
        input_output_aliases={5: 0} if earlier else {},
        cost_estimate=pl.CostEstimate(
            flops=6 * pairs * 256 * 256 * 256, bytes_accessed=3 * half * pairs * PAIR * 4, transcendentals=0
        ),
        compiler_params=pltpu.CompilerParams(vmem_limit_bytes=16 * MIB),
        interpret=INTERPRET,
        name="bubble_along_y",
    )(propagator, mirror, flip, high, low, *earlier, *after)


def whole(array):
    return pl.BlockSpec(array.shape, lambda *i: (0,) * array.ndim, pipeline_mode=pl.Buffered(1))


def along_x_kernel(first, span, copies, counts, *refs):
    parts, (high_ref, low_ref), out_ref = refs[: len(counts)], refs[len(counts) : len(counts) + 2], refs[-1]
    table = (high_ref[...], low_ref[...])
    first_half = lax.broadcasted_iota(jnp.int32, (HALF_L, LANES), 1) < LANES // 2
    start = first + pl.program_id(0) * span

    def lines(ky):
        return jnp.concatenate(
            [
                part[pl.ds(offset + ky, count, stride=256), :]
                for offset in (0, 128)
                for part, count in zip(parts, counts)
            ],
            axis=0,
        )

    for m in range(0, span, 2):
        both = jnp.concatenate([lines(start + m), lines(start + m + 1)], axis=1)
        result = product3(table, halves_of(both), NN)
        for v in range(2):
            even = result[:HALF_L, LANES * v : LANES * (v + 1)]
            odd = result[HALF_L:, LANES * v : LANES * (v + 1)]
            both_halves = jnp.where(first_half, even + lane_swap(odd), lane_swap(even) - odd)
            for copy in range(copies):
                out_ref[copy, (m + v) * HALF_L : (m + v + 1) * HALF_L, :] = both_halves


def along_x(parts, first, span, rows, copies, after):
    counts = tuple(p.shape[0] for p in parts)
    high, low = along_x_table(sum(counts))
    flat = [p.reshape(-1, LANES) for p in parts]
    block = span * HALF_L
    return pl.pallas_call(
        lambda *refs: along_x_kernel(first, span, copies, counts, *refs),
        grid=(-(-rows // block),),
        in_specs=[whole(a) for a in (*flat, high, low)] + [anywhere] * len(after),
        out_specs=pl.BlockSpec((copies, block, LANES), lambda i: (0, i, 0)),
        out_shape=jax.ShapeDtypeStruct((copies, rows, LANES), f32),
        cost_estimate=pl.CostEstimate(
            flops=6 * rows * 2 * 256 * LANES, bytes_accessed=12 * 1024 * 1024, transcendentals=0
        ),
        compiler_params=pltpu.CompilerParams(vmem_limit_bytes=20 * MIB),
        interpret=INTERPRET,
        name="along_x",
    )(*flat, high, low, *after)


def gathered(x, lane):
    return jnp.take_along_axis(x, lane, axis=1, mode="promise_in_bounds")


def frequency_kernel(both_sides, sign_ref, x_ref, bare_ref, *refs):
    tables, out_ref = refs[:8], refs[-1]
    forth = ((tables[0][...], tables[1][...]), (tables[2][...], tables[3][...]))
    back = ((tables[4][...], tables[5][...]), (tables[6][...], tables[7][...]))
    hs = x_ref.shape[0] // 2
    tile = x_ref.shape[1:]
    lane = lax.broadcasted_iota(jnp.int32, tile, 1)
    first_half = lane < LANES // 2
    mixed = [
        [x_ref[k] + x_ref[k + hs] for k in range(hs)],
        [x_ref[k] - x_ref[k + hs] for k in range(hs)],
    ]
    for side in range(2):
        bare = bare_ref[side]
        result = []
        for parity in range(2):
            u = mixed[parity]
            pieces = []
            for k in range(0, hs, 2):
                if side == 0:
                    pieces.append(jnp.where(first_half, u[k], lane_swap(u[k + 1])))
                else:
                    pieces.append(jnp.where(first_half, lane_swap(u[k]), u[k + 1]))
            pol = product3(halves_of(jnp.concatenate(pieces, axis=1)), forth[parity], NN)
            screened = bare * bare * pol / jnp.maximum(1.0 - bare * pol, 1.0)
            if parity == 0:
                zero = lax.broadcasted_iota(jnp.int32, screened.shape, 1) == 0
                screened = jnp.where(zero, 0.5 * screened, screened)
            result.append(product3(halves_of(screened), back[parity], NN))
        for d in range(hs // 2):
            lanes = slice(LANES * d, LANES * (d + 1))
            even, odd = result[0][:, lanes], result[1][:, lanes]
            if not both_sides:
                odd = odd * sign_ref[0]
            near, far = even + odd, even - odd
            out_ref[d, side] = near
            out_ref[hs - 1 - d, side] = gathered(far, LANES - 1 - lane)
            if both_sides:
                out_ref[hs + d, side] = far
                out_ref[2 * hs - 1 - d, side] = gathered(near, LANES - 1 - lane)


def through_frequencies(x, bare, tables, block, sign, both_sides, after):
    sources, rows, _ = x.shape
    slabs = sources if both_sides else sources // 2
    return pl.pallas_call(
        lambda *refs: frequency_kernel(both_sides, *refs),
        grid=(-(-rows // block),),
        in_specs=[
            pl.BlockSpec(memory_space=pltpu.SMEM),
            pl.BlockSpec((sources, block, LANES), lambda i: (0, i, 0)),
            pl.BlockSpec((2, block, 1), lambda i: (0, i, 0)),
        ]
        + [whole(a) for a in tables]
        + [anywhere] * len(after),
        out_specs=pl.BlockSpec((slabs, 2, block, LANES), lambda i: (0, 0, i, 0)),
        out_shape=jax.ShapeDtypeStruct((slabs, 2, rows, LANES), f32),
        cost_estimate=pl.CostEstimate(
            flops=48 * rows * 512 * 512, bytes_accessed=3 * x.size * 4, transcendentals=0
        ),
        interpret=INTERPRET,
        name="through_frequencies",
    )(sign, x, bare, *tables, *after)


def line_order():
    return np.concatenate([np.arange(1, KEPT), [0]])


def back_x_table():
    table = np.zeros((2 * ROWS_X, L))
    angle = np_angle(line_order(), np.arange(L))
    table[:KEPT] = np.cos(angle) / L
    table[ROWS_X : ROWS_X + KEPT] = np.sin(angle) / L
    return table_halves(table)


def back_x_kernel(count, depth, sines, *refs):
    lower_ref, upper_ref, high_ref, low_ref, z_ref = refs
    flat = [r.reshape(r.shape[0] * r.shape[1], LANES) for r in (lower_ref, upper_ref)]
    back_x(count, depth, sines, flat, high_ref, low_ref, z_ref)


def gather_back_x_kernel(sources, count, depth, sines, own_ref, *refs):
    blocks, (high_ref, low_ref), (z_ref, flat_ref) = refs[:sources], refs[sources : sources + 2], refs[-2:]
    rows = blocks[0].shape[1]
    for k, block in enumerate(blocks):
        place = pl.ds(pl.multiple_of((own_ref[0] ^ k) * rows, 8), rows)
        for side in range(2):
            flat_ref[side, place, :] = block[side]
    back_x(count, depth, sines, [flat_ref.at[0], flat_ref.at[1]], high_ref, low_ref, z_ref)


def back_x(count, depth, sines, flat, high_ref, low_ref, z_ref):
    table = (high_ref[...], low_ref[...])
    z_ref[...] = jnp.zeros_like(z_ref)

    def lines(ky):
        rows = pl.ds(ky * HALF_L, HALF_L)
        return jnp.concatenate([flat[0][rows, :], flat[1][rows, :]], axis=0)

    def put(ky, result):
        z_ref[pl.ds(ky, KEPT, stride=depth), :] = result[:KEPT]
        z_ref[pl.ds(sines + ky, KEPT, stride=depth), :] = result[ROWS_X : ROWS_X + KEPT]

    def pair(ky):
        both = jnp.concatenate([lines(ky), lines(ky + 1)], axis=1)
        result = product3(table, halves_of(both), NN)
        put(ky, result[:, :LANES])
        put(ky + 1, result[:, LANES:])

    unrolled = 4

    def body(m, carry):
        for v in range(unrolled):
            pair(2 * (unrolled * m + v))
        return carry

    lax.fori_loop(0, count // (2 * unrolled), body, 0)
    for ky in range(count // (2 * unrolled) * 2 * unrolled, count - 1, 2):
        pair(ky)
    if count % 2:
        put(count - 1, product3(table, halves_of(lines(count - 1)), NN))


def back_x_depth(count):
    sines = -(-count // 8) * 8
    return sines, (2 * sines // 8 | 1) * 8


def back_along_x(w, count):
    sources, _, rows, _ = w.shape
    high, low = back_x_table()
    sines, depth = back_x_depth(count)
    side = lambda s: pl.BlockSpec(
        (sources, None, rows, LANES), lambda i: (0, s, 0, 0), pipeline_mode=pl.Buffered(1)
    )
    return pl.pallas_call(
        lambda *refs: back_x_kernel(count, depth, sines, *refs),
        grid=(1,),
        in_specs=[side(0), side(1), whole(high), whole(low)],
        out_specs=pl.BlockSpec((KEPT * depth, LANES), lambda i: (0, 0)),
        out_shape=jax.ShapeDtypeStruct((KEPT * depth, LANES), f32),
        cost_estimate=pl.CostEstimate(
            flops=6 * count * 256 * 256 * LANES, bytes_accessed=10 * 1024 * 1024, transcendentals=0
        ),
        compiler_params=pltpu.CompilerParams(vmem_limit_bytes=24 * MIB),
        interpret=INTERPRET,
        name="back_along_x",
    )(w, w, high, low)


def gather_back_along_x(blocks, own, count, after):
    _, rows, _ = blocks[0].shape
    high, low = back_x_table()
    sines, depth = back_x_depth(count)
    return pl.pallas_call(
        lambda *refs: gather_back_x_kernel(len(blocks), count, depth, sines, *refs),
        grid=(1,),
        in_specs=[pl.BlockSpec(memory_space=pltpu.SMEM)] + [whole(a) for a in (*blocks, high, low)]
        + [anywhere] * len(after),
        out_specs=pl.BlockSpec((KEPT * depth, LANES), lambda i: (0, 0)),
        out_shape=jax.ShapeDtypeStruct((KEPT * depth, LANES), f32),
        scratch_shapes=[pltpu.VMEM((2, len(blocks) * rows, LANES), f32)],
        cost_estimate=pl.CostEstimate(
            flops=6 * count * 256 * 256 * LANES, bytes_accessed=10 * 1024 * 1024, transcendentals=0
        ),
        compiler_params=pltpu.CompilerParams(vmem_limit_bytes=24 * MIB),
        interpret=INTERPRET,
        name="gather_back_along_x",
    )(own, *blocks, high, low, *after)


def back_y_table(first, chunks):
    tables = []
    y = np.arange(LANES)
    for count in chunks:
        sines, depth = back_x_depth(count)
        ky = np.arange(first, first + count)
        angle = np_angle(ky, y)
        table = np.zeros((depth, 2 * LANES))
        table[:count, :LANES] = np_twice(ky)[:, None] * np.cos(angle)
        table[sines : sines + count, LANES:] = np_twice(ky)[:, None] * np.sin(angle)
        tables.append(table)
        first += count
    return table_halves(np.concatenate(tables, axis=0))


X_STEP = 32


def turned_lines(parts, table):
    result = product3(halves_of(jnp.concatenate(parts, axis=0).T), table, NN)
    cosines, sines = result[:, :LANES], result[:, LANES:]
    return cosines - sines, cosines + sines


def partial_back_y_kernel(depths, *refs):
    blocks, (high_ref, low_ref, minus_ref, plus_ref) = refs[:-4], refs[-4:]
    table = (high_ref[...], low_ref[...])
    for s in range(minus_ref.shape[0]):
        lines = [r[s * d : (s + 1) * d, :] for r, d in zip(blocks, depths)]
        minus_ref[s], plus_ref[s] = turned_lines(lines, table)


def partial_back_along_y(parts, chunks):
    high, low = back_y_table(0, chunks)
    depths = tuple(back_x_depth(c)[1] for c in chunks)
    step = 8
    line = jax.ShapeDtypeStruct((KEPT, LANES, LANES), f32)
    return pl.pallas_call(
        lambda *refs: partial_back_y_kernel(depths, *refs),
        grid=(-(-KEPT // step),),
        in_specs=[pl.BlockSpec((step * d, LANES), lambda i: (i, 0)) for d in depths] + [whole(high), whole(low)],
        out_specs=[pl.BlockSpec((step, LANES, LANES), lambda i: (i, 0, 0))] * 2,
        out_shape=[line, line],
        cost_estimate=pl.CostEstimate(
            flops=6 * KEPT * 128 * 256 * 256, bytes_accessed=24 * MIB, transcendentals=0
        ),
        interpret=INTERPRET,
        name="partial_back_along_y",
    )(*parts, high, low)


def back_y_kernel(depth, *refs):
    halves, heads, zeroth = refs[:3], refs[3:6], refs[6:9]
    high_ref, low_ref, own_ref, out_ref, minus_ref, plus_ref = refs[9:]
    step, side = pl.program_id(0), pl.program_id(1)
    table = (high_ref[...], low_ref[...])
    lane = lax.broadcasted_iota(jnp.int32, (LANES, LANES), 1)
    turned_lane = (LANES // 2 - lane) & (LANES - 1)
    ring = 2 * X_STEP

    def fill(source, s, line):
        z_ref, early_minus_ref, early_plus_ref = source
        minus, plus = turned_lines([z_ref[s * depth : (s + 1) * depth, :]], table)
        slot = line & (ring - 1)
        minus_ref[slot] = minus + early_minus_ref[s]
        plus_ref[slot] = plus + early_plus_ref[s]

    @pl.when((step == 0) & (side == 0))
    def _():
        fill(zeroth, 0, step)
        for s in range(X_STEP // 2):
            fill(heads, s, step + 1 + s)

    half = jnp.minimum(2 * step + 1 + side, 2 * HALF_L // X_STEP - 1)
    for s in range(X_STEP // 2):
        fill(halves, s, half * (X_STEP // 2) + 1 + s)

    def emit(near_ref, far_ref, offsets):
        slots = [(step * X_STEP + s) & (ring - 1) for s in offsets]
        for u in range(X_STEP // 2):
            even, odd = slots[2 * u], slots[2 * u + 1]
            near = near_ref[even]
            far = gathered(far_ref[even], turned_lane)
            near_odd = lane_swap(near_ref[odd])
            far_odd = lane_swap(gathered(far_ref[odd], turned_lane))
            tiles = (
                jnp.where(lane <= HALF_L, near, far),
                jnp.where(lane < LANES // 2, far, near_odd),
                jnp.where(lane <= HALF_L - LANES // 2, near_odd, far_odd),
            )
            for i, w in enumerate(tiles):
                lanes = slice(u * PAIR + i * LANES, u * PAIR + (i + 1) * LANES)
                out_ref[:, lanes] = -own_ref[:, lanes] * w

    @pl.when(side == 0)
    def _():
        emit(minus_ref, plus_ref, range(X_STEP))

    @pl.when(side == 1)
    def _():
        emit(plus_ref, minus_ref, range(X_STEP, 0, -1))


def back_along_y(propagator, early, last, first, count):
    slab, sites = propagator.shape
    high, low = back_y_table(first, [count])
    depth = back_x_depth(count)[1]
    width = X_STEP * L
    steps = HALF_L // X_STEP
    half = X_STEP // 2
    moving = pl.BlockSpec((slab, width), lambda i, j: (0, jnp.where(j == 0, i, 2 * steps - 1 - i)))

    def lines(size, index):
        return [pl.BlockSpec((size * depth, LANES), lambda i, j: (index(i, j), 0))] + [
            pl.BlockSpec((size, LANES, LANES), lambda i, j: (index(i, j), 0, 0))
        ] * 2

    sources = (last, *early)
    return pl.pallas_call(
        lambda *refs: back_y_kernel(depth, *refs),
        grid=(steps, 2),
        in_specs=lines(half, lambda i, j: jnp.minimum(2 * i + 1 + j, 2 * steps - 1))
        + lines(half, lambda i, j: 0)
        + lines(1, lambda i, j: HALF_L)
        + [whole(high), whole(low), moving],
        out_specs=moving,
        out_shape=jax.ShapeDtypeStruct((slab, sites), f32),
        scratch_shapes=[pltpu.VMEM((2 * X_STEP, LANES, LANES), f32)] * 2,
        cost_estimate=pl.CostEstimate(
            flops=6 * KEPT * 128 * 256 * 256, bytes_accessed=2 * propagator.size * 4, transcendentals=0
        ),
        interpret=INTERPRET,
        name="back_along_y",
    )(*sources, *sources, *sources, high, low, propagator)


CUTS = (0, 40, KEPT // 2 + 1)
CHUNKS = ((32, 8, 96, False), (33, 12, 200, True), (32, 8, 96, False))


def token(x):
    return lax.slice(x.reshape(-1, LANES), (0, 0), (8, LANES))


def chunk_firsts():
    return [sum(c[0] for c in CHUNKS[:i]) for i in range(len(CHUNKS))]


def pick_kernel(own_ref, w_ref, *refs):
    slabs = w_ref.shape[0]
    for k, out_ref in enumerate(refs[-slabs:]):
        out_ref[...] = w_ref[own_ref[0] ^ k]


def picked(w, own, after):
    shape = w.shape[1:]
    return list(
        pl.pallas_call(
            pick_kernel,
            grid=(1,),
            in_specs=[pl.BlockSpec(memory_space=pltpu.SMEM), whole(w)] + [anywhere] * len(after),
            out_specs=[pl.BlockSpec(shape, lambda i: (0, 0, 0))] * w.shape[0],
            out_shape=[jax.ShapeDtypeStruct(shape, f32)] * w.shape[0],
            cost_estimate=pl.CostEstimate(flops=0, bytes_accessed=8 * w.size, transcendentals=0),
            compiler_params=pltpu.CompilerParams(vmem_limit_bytes=16 * MIB),
            interpret=INTERPRET,
            name="picked",
        )(own, w, *after)
    )


def frequency_tables(points, slab):
    half = slab // 2
    quarter = points // 4
    slot = lax.optimization_barrier(jnp.arange(quarter, dtype=jnp.int32))
    count = lax.optimization_barrier(jnp.arange(NF // 2, dtype=jnp.int32))
    held = slot // half * slab + slot % half
    tables = []
    for times, turned in ((held, False), (slot, True)):
        for parity in (0, 1):
            n = 2 * count + parity
            a, b = (n[:, None], times[None, :]) if turned else (n[None, :], times[:, None])
            phase = a * (2 * b + 1) % (2 * points)
            table = jnp.cos(jnp.pi * phase.astype(f32) / points) * (2.0 / math.sqrt(points))
            high = lax.reduce_precision(table, 8, 7)
            tables += [high.astype(bf16), (table - high).astype(bf16)]
    return tables


def with_kernels(propagator, onsite_coupling, neighbour_strength):
    devices = lax.axis_size("tau")
    me = lax.axis_index("tau")
    slab, _ = propagator.shape
    half = slab // 2

    partner = [(d, devices - 1 - d) for d in range(devices)]
    tables = frequency_tables(slab * devices, slab)
    lines = None
    for first, last in zip(CUTS[:-1], CUTS[1:]):
        mirror = lax.ppermute(propagator[half:, first * PAIR : last * PAIR], "tau", partner)
        lines = bubble_along_y(propagator, mirror, first, last - first, lines, [] if first else tables)

    sides = devices // 2
    own = (me % sides)[None].astype(jnp.int32)
    sign = jnp.where(me < sides, 1.0, -1.0)[None].astype(f32)
    firsts = chunk_firsts()
    moved, turned = [], []
    for i, (first, (count, span, block, shared)) in enumerate(zip(firsts, CHUNKS)):
        owners = sides if shared else devices
        rows = -(-count * HALF_L // (8 * owners)) * 8
        pol_mom = along_x([lines], first, span, rows * owners, devices // owners, [token(m) for m in moved[-1:]] + [token(w) for w in turned[: max(i - 1, 0)]])
        moved.append(pol_mom)
        pol_mom = pol_mom.reshape(devices, rows, LANES)
        by_momentum = lax.all_to_all(pol_mom, "tau", split_axis=0, concat_axis=0, tiled=True)
        row = me % owners * rows + jnp.arange(rows, dtype=jnp.int32)
        bare = jnp.stack(
            [
                bare_potential(
                    row % HALF_L + HALF_L * side, first + row // HALF_L, onsite_coupling[0], neighbour_strength[0]
                )
                for side in (0, 1)
            ]
        )[:, :, None]
        turned.append(through_frequencies(by_momentum, bare, tables, block, sign, not shared, [token(w) for w in turned[-1:]]))

    def exchanged(blocks):
        for k in range(1, len(blocks)):
            blocks[k] = lax.ppermute(blocks[k], "tau", [(d, d ^ k) for d in range(devices)])
        return blocks

    returned = []
    counts = [c[0] for c in CHUNKS]
    for first, (count, _, _, shared), w in zip(firsts, CHUNKS, turned):
        if shared:
            blocks = exchanged(picked(w, own, []))
            returned.append(gather_back_along_x(blocks, own, count, []))
        elif w is turned[-1]:
            place = me[None].astype(jnp.int32)
            blocks = exchanged(picked(w, place, []))
            early = partial_back_along_y(returned, counts[:-1])
            last = gather_back_along_x(blocks, place, count, [token(e) for e in early])
        else:
            w = lax.all_to_all(w, "tau", split_axis=0, concat_axis=0, tiled=True)
            returned.append(back_along_x(w, count))
    return back_along_y(propagator, early, last, firsts[-1], counts[-1])


def per_device(propagator, onsite_coupling, neighbour_strength):
    slab, sites = propagator.shape
    devices = lax.axis_size("tau")
    fits = slab == LANES and sites == L * L and 4 * NF == 2 * slab * devices and devices & (devices - 1) == 0
    run = with_kernels if fits else plain
    return run(propagator, onsite_coupling, neighbour_strength)


def solution(mesh):
    in_specs = (P(("grp", "tau"), None), P("grp"), P("grp"))
    out_specs = P(("grp", "tau"), None)
    return jax.shard_map(
        per_device, mesh=mesh, in_specs=in_specs, out_specs=out_specs, check_vma=False
    )
```

```python
import math

import jax
import jax.numpy as jnp
import numpy as np
from jax import lax
from jax.experimental import pallas as pl
from jax.experimental.pallas import tpu as pltpu
from jax.sharding import PartitionSpec as P


L = 192
NF = 1024

mode = lax.Precision.HIGH


def cos_table(rows, columns, period):
    phase = rows[:, None] * columns[None, :] % period
    return jnp.cos(2.0 * jnp.pi * phase.astype(jnp.float32) / period)


def sin_table(rows, columns, period):
    phase = rows[:, None] * columns[None, :] % period
    return jnp.sin(2.0 * jnp.pi * phase.astype(jnp.float32) / period)


def time_table(times, points):
    frequency = jnp.arange(NF, dtype=jnp.int32)[None, :]
    phase = frequency * (2 * times[:, None] + 1) % (2 * points)
    return jnp.cos(jnp.pi * phase.astype(jnp.float32) / points) / math.sqrt(points)


def bare_potential(first, second, onsite, nearest):
    first = first.astype(jnp.float32)
    second = second.astype(jnp.float32)
    return onsite + 2.0 * nearest * (
        jnp.cos(2.0 * jnp.pi * first / L) + jnp.cos(2.0 * jnp.pi * second / L)
    )


def screen(pol_mom, bare):
    denom = jnp.maximum(1.0 - bare * pol_mom, 1.0)
    return bare * bare * pol_mom / denom


def plain(propagator, onsite_coupling, neighbour_strength):
    devices = lax.axis_size("tau")
    slab, sites = propagator.shape
    half = slab // 2
    points = slab * devices
    kept = L // 2 + 1
    width = kept * L
    block = -(-width // (8 * devices)) * 8
    padded = block * devices

    waves = jnp.arange(L, dtype=jnp.int32)
    halves = jnp.arange(kept, dtype=jnp.int32)
    twice = jnp.where((halves == 0) | (halves == L // 2), 1.0, 2.0).astype(jnp.float32)

    partner = [(d, devices - 1 - d) for d in range(devices)]
    mirrored = lax.ppermute(propagator[half:, :width], "tau", partner)
    polarization = -propagator[:half, :width] * mirrored[::-1]

    field = polarization.reshape(half, kept, L)
    along_cos = cos_table(halves, waves, L) / L
    along_sin = sin_table(halves, waves, L) / L
    first_cos = jnp.einsum("fxy,ly->fxl", field, along_cos, precision=mode)
    first_sin = jnp.einsum("fxy,ly->fxl", field, along_sin, precision=mode)
    cos_x = cos_table(waves, halves, L)
    sin_x = sin_table(waves, halves, L)
    pol_mom = jnp.einsum("fxl,kx->flk", first_cos, cos_x * twice, precision=mode) - jnp.einsum(
        "fxl,kx->flk", first_sin, sin_x * twice, precision=mode
    )
    pol_mom = jnp.pad(pol_mom.reshape(half, width), ((0, 0), (0, padded - width)))
    by_momentum = lax.all_to_all(pol_mom, "tau", split_axis=1, concat_axis=0, tiled=True)

    held = jnp.arange(devices * half, dtype=jnp.int32)
    times = held // half * slab + held % half
    forward = 2.0 * time_table(times, points)
    pol_freq = jnp.einsum("tn,tq->nq", forward, by_momentum, precision=mode)
    momenta = lax.axis_index("tau") * block + jnp.arange(block, dtype=jnp.int32)
    bare = bare_potential(momenta % L, momenta // L, onsite_coupling[0], neighbour_strength[0])
    screened = screen(pol_freq, bare[None, :])
    weight = jnp.where(jnp.arange(NF) == 0, 1.0, 2.0).astype(jnp.float32)
    inverse = time_table(jnp.arange(points, dtype=jnp.int32), points) * weight
    w_columns = jnp.einsum("tn,nq->tq", inverse, screened, precision=mode)

    back = lax.all_to_all(w_columns, "tau", split_axis=0, concat_axis=1, tiled=True)
    back = back[:, :width].reshape(slab, kept, L)
    back_cos = jnp.einsum("flk,kx->flx", back, cos_table(waves, waves, L) / L, precision=mode)
    back_sin = jnp.einsum("flk,kx->flx", back, sin_table(waves, waves, L) / L, precision=mode)
    w_time = jnp.einsum("flx,yl->fxy", back_cos, cos_table(waves, halves, L) * twice, precision=mode) - jnp.einsum(
        "flx,yl->fxy", back_sin, sin_table(waves, halves, L) * twice, precision=mode
    )
    return -propagator * w_time.reshape(slab, sites)


LANES = 128
PAIR = 2 * L
HALF_L = L // 2
KEPT = HALF_L + 1
ROWS_X = 104
INTERPRET = False
MIB = 1024 * 1024
bf16 = jnp.bfloat16
f32 = jnp.float32
NN = (((1,), (0,)), ((), ()))
NT = (((1,), (1,)), ((), ()))


def halves_of(x):
    high = x.astype(bf16)
    return high, (x - high.astype(f32)).astype(bf16)


def product(a, b, dims):
    return lax.dot_general(a, b, dims, preferred_element_type=f32)


def product3(a, b, dims):
    return product(a[0], b[0], dims) + product(a[0], b[1], dims) + product(a[1], b[0], dims)


def table_halves(table):
    high = np.asarray(table, np.float32).astype(bf16)
    low = (np.asarray(table, np.float64) - high.astype(np.float64)).astype(np.float32).astype(bf16)
    return jnp.asarray(high), jnp.asarray(low)


def np_angle(a, b):
    return 2.0 * np.pi * ((a[:, None] * b[None, :]) % L) / L


def np_twice(a):
    return np.where((a == 0) | (a == HALF_L), 1.0, np.where(a > HALF_L, 0.0, 2.0))


def along_y_table():
    table = np.zeros((256, 512))
    angle = np_angle(np.arange(KEPT), np.arange(L))
    for i, part in enumerate((np.cos(angle), np.sin(angle))):
        table[128 * i : 128 * i + KEPT, 0:L] = part / L
        table[128 * i : 128 * i + KEPT, 256 + 64 : 512] = part / L
    return table_halves(table)


def along_x_table(pairs):
    table = np.zeros((L, 2 * pairs))
    for parity in (0, 1):
        x = 2 * np.arange(pairs) + parity
        angle = np_angle(np.arange(HALF_L), x)
        rows = slice(HALF_L * parity, HALF_L * (parity + 1))
        table[rows, :pairs] = np.cos(angle) * np_twice(x)
        table[rows, pairs:] = -np.sin(angle) * np_twice(x)
    return table_halves(table)


anywhere = pl.BlockSpec(memory_space=pl.ANY)


def lane_swap(x):
    return pltpu.roll(x, LANES // 2, 1)


GROUP = 8


def bubble_kernel(limit, own_ref, mirror_ref, flip_ref, high_ref, low_ref, out_ref):
    start = pl.program_id(0) * GROUP
    table = (high_ref[...], low_ref[...])
    flip = flip_ref[...]
    first_half = lax.broadcasted_iota(jnp.int32, (256, LANES), 1) < LANES // 2
    for u in range(0, GROUP, 4):
        lines = []
        for v in range(u, u + 4, 2):
            lanes = slice(v * PAIR, (v + 2) * PAIR)
            high, low = halves_of(mirror_ref[:, lanes])
            mirrored = product(flip, high, NN) + product(flip, low, NN)
            field = -own_ref[:, lanes] * mirrored
            lines += [field[:, :PAIR], field[:, PAIR:]]
        lines = [jnp.where(start + u + i < limit, line, 0.0) for i, line in enumerate(lines)]
        even = jnp.concatenate([line[:, :256] for line in lines], axis=0)
        odd = jnp.concatenate([line[:, 128:] for line in lines], axis=0)
        even = product3((table[0][:, :256], table[1][:, :256]), halves_of(even), NT)
        odd = product3((table[0][:, 256:], table[1][:, 256:]), halves_of(odd), NT)
        for v in range(2):
            lanes = slice(v * LANES, (v + 1) * LANES)
            near, far = even[:, lanes], odd[:, lanes]
            out_ref[u + 2 * v] = jnp.where(first_half, near, lane_swap(far))
            out_ref[u + 2 * v + 1] = jnp.where(first_half, lane_swap(near), far)


def bubble_along_y(propagator, mirror, first, pairs, before, after):
    half = propagator.shape[0] // 2
    steps = -(-pairs // GROUP)
    shift = first // GROUP
    width = GROUP * PAIR
    high, low = along_y_table()
    flip = jnp.asarray(np.eye(half)[::-1].astype(bf16))
    whole = lambda a: pl.BlockSpec(a.shape, lambda i: (0,) * a.ndim)
    total = -(-(KEPT // 2 + 1) // GROUP) * GROUP
    earlier = [] if before is None else [before]
    return pl.pallas_call(
        lambda *refs: bubble_kernel(pairs, *refs[:5], refs[-1]),
        grid=(steps,),
        in_specs=[
            pl.BlockSpec((half, width), lambda i: (0, i + shift)),
            pl.BlockSpec((half, width), lambda i: (0, i)),
            whole(flip),
            whole(high),
            whole(low),
        ]
        + [anywhere] * (len(earlier) + len(after)),
        out_specs=pl.BlockSpec((GROUP, 256, LANES), lambda i: (i + shift, 0, 0)),
        out_shape=jax.ShapeDtypeStruct((total, 256, LANES), f32),
        input_output_aliases={5: 0} if earlier else {},
        cost_estimate=pl.CostEstimate(
            flops=6 * pairs * 256 * 256 * 256, bytes_accessed=3 * half * pairs * PAIR * 4, transcendentals=0
        ),
        compiler_params=pltpu.CompilerParams(vmem_limit_bytes=16 * MIB),
        interpret=INTERPRET,
        name="bubble_along_y",
    )(propagator, mirror, flip, high, low, *earlier, *after)


def whole(array):
    return pl.BlockSpec(array.shape, lambda *i: (0,) * array.ndim, pipeline_mode=pl.Buffered(1))


def along_x_kernel(first, span, copies, counts, *refs):
    parts, (high_ref, low_ref), out_ref = refs[: len(counts)], refs[len(counts) : len(counts) + 2], refs[-1]
    table = (high_ref[...], low_ref[...])
    first_half = lax.broadcasted_iota(jnp.int32, (HALF_L, LANES), 1) < LANES // 2
    start = first + pl.program_id(0) * span

    def lines(ky):
        return jnp.concatenate(
            [
                part[pl.ds(offset + ky, count, stride=256), :]
                for offset in (0, 128)
                for part, count in zip(parts, counts)
            ],
            axis=0,
        )

    for m in range(0, span, 2):
        both = jnp.concatenate([lines(start + m), lines(start + m + 1)], axis=1)
        result = product3(table, halves_of(both), NN)
        for v in range(2):
            even = result[:HALF_L, LANES * v : LANES * (v + 1)]
            odd = result[HALF_L:, LANES * v : LANES * (v + 1)]
            both_halves = jnp.where(first_half, even + lane_swap(odd), lane_swap(even) - odd)
            for copy in range(copies):
                out_ref[copy, (m + v) * HALF_L : (m + v + 1) * HALF_L, :] = both_halves


def along_x(parts, first, span, rows, copies, after):
    counts = tuple(p.shape[0] for p in parts)
    high, low = along_x_table(sum(counts))
    flat = [p.reshape(-1, LANES) for p in parts]
    block = span * HALF_L
    return pl.pallas_call(
        lambda *refs: along_x_kernel(first, span, copies, counts, *refs),
        grid=(-(-rows // block),),
        in_specs=[whole(a) for a in (*flat, high, low)] + [anywhere] * len(after),
        out_specs=pl.BlockSpec((copies, block, LANES), lambda i: (0, i, 0)),
        out_shape=jax.ShapeDtypeStruct((copies, rows, LANES), f32),
        cost_estimate=pl.CostEstimate(
            flops=6 * rows * 2 * 256 * LANES, bytes_accessed=12 * 1024 * 1024, transcendentals=0
        ),
        compiler_params=pltpu.CompilerParams(vmem_limit_bytes=20 * MIB),
        interpret=INTERPRET,
        name="along_x",
    )(*flat, high, low, *after)


def gathered(x, lane):
    return jnp.take_along_axis(x, lane, axis=1, mode="promise_in_bounds")


def frequency_kernel(both_sides, sign_ref, x_ref, bare_ref, *refs):
    tables, out_ref = refs[:8], refs[-1]
    forth = ((tables[0][...], tables[1][...]), (tables[2][...], tables[3][...]))
    back = ((tables[4][...], tables[5][...]), (tables[6][...], tables[7][...]))
    hs = x_ref.shape[0] // 2
    tile = x_ref.shape[1:]
    lane = lax.broadcasted_iota(jnp.int32, tile, 1)
    first_half = lane < LANES // 2
    mixed = [
        [x_ref[k] + x_ref[k + hs] for k in range(hs)],
        [x_ref[k] - x_ref[k + hs] for k in range(hs)],
    ]
    for side in range(2):
        bare = bare_ref[side]
        result = []
        for parity in range(2):
            u = mixed[parity]
            pieces = []
            for k in range(0, hs, 2):
                if side == 0:
                    pieces.append(jnp.where(first_half, u[k], lane_swap(u[k + 1])))
                else:
                    pieces.append(jnp.where(first_half, lane_swap(u[k]), u[k + 1]))
            pol = product3(halves_of(jnp.concatenate(pieces, axis=1)), forth[parity], NN)
            screened = bare * bare * pol / jnp.maximum(1.0 - bare * pol, 1.0)
            if parity == 0:
                zero = lax.broadcasted_iota(jnp.int32, screened.shape, 1) == 0
                screened = jnp.where(zero, 0.5 * screened, screened)
            result.append(product3(halves_of(screened), back[parity], NN))
        for d in range(hs // 2):
            lanes = slice(LANES * d, LANES * (d + 1))
            even, odd = result[0][:, lanes], result[1][:, lanes]
            if not both_sides:
                odd = odd * sign_ref[0]
            near, far = even + odd, even - odd
            out_ref[d, side] = near
            out_ref[hs - 1 - d, side] = gathered(far, LANES - 1 - lane)
            if both_sides:
                out_ref[hs + d, side] = far
                out_ref[2 * hs - 1 - d, side] = gathered(near, LANES - 1 - lane)


def through_frequencies(x, bare, tables, block, sign, both_sides, after):
    sources, rows, _ = x.shape
    slabs = sources if both_sides else sources // 2
    return pl.pallas_call(
        lambda *refs: frequency_kernel(both_sides, *refs),
        grid=(-(-rows // block),),
        in_specs=[
            pl.BlockSpec(memory_space=pltpu.SMEM),
            pl.BlockSpec((sources, block, LANES), lambda i: (0, i, 0)),
            pl.BlockSpec((2, block, 1), lambda i: (0, i, 0)),
        ]
        + [whole(a) for a in tables]
        + [anywhere] * len(after),
        out_specs=pl.BlockSpec((slabs, 2, block, LANES), lambda i: (0, 0, i, 0)),
        out_shape=jax.ShapeDtypeStruct((slabs, 2, rows, LANES), f32),
        cost_estimate=pl.CostEstimate(
            flops=48 * rows * 512 * 512, bytes_accessed=3 * x.size * 4, transcendentals=0
        ),
        interpret=INTERPRET,
        name="through_frequencies",
    )(sign, x, bare, *tables, *after)


def line_order():
    return np.concatenate([np.arange(1, KEPT), [0]])


def back_x_table():
    table = np.zeros((2 * ROWS_X, L))
    angle = np_angle(line_order(), np.arange(L))
    table[:KEPT] = np.cos(angle) / L
    table[ROWS_X : ROWS_X + KEPT] = np.sin(angle) / L
    return table_halves(table)


def back_x_kernel(count, depth, sines, *refs):
    lower_ref, upper_ref, high_ref, low_ref, z_ref = refs
    flat = [r.reshape(r.shape[0] * r.shape[1], LANES) for r in (lower_ref, upper_ref)]
    back_x(count, depth, sines, flat, high_ref, low_ref, z_ref)


def gather_back_x_kernel(sources, count, depth, sines, own_ref, *refs):
    blocks, (high_ref, low_ref), (z_ref, flat_ref) = refs[:sources], refs[sources : sources + 2], refs[-2:]
    rows = blocks[0].shape[1]
    for k, block in enumerate(blocks):
        place = pl.ds(pl.multiple_of((own_ref[0] ^ k) * rows, 8), rows)
        for side in range(2):
            flat_ref[side, place, :] = block[side]
    back_x(count, depth, sines, [flat_ref.at[0], flat_ref.at[1]], high_ref, low_ref, z_ref)


def back_x(count, depth, sines, flat, high_ref, low_ref, z_ref):
    table = (high_ref[...], low_ref[...])
    z_ref[...] = jnp.zeros_like(z_ref)

    def lines(ky):
        rows = pl.ds(ky * HALF_L, HALF_L)
        return jnp.concatenate([flat[0][rows, :], flat[1][rows, :]], axis=0)

    def put(ky, result):
        z_ref[pl.ds(ky, KEPT, stride=depth), :] = result[:KEPT]
        z_ref[pl.ds(sines + ky, KEPT, stride=depth), :] = result[ROWS_X : ROWS_X + KEPT]

    def pair(ky):
        both = jnp.concatenate([lines(ky), lines(ky + 1)], axis=1)
        result = product3(table, halves_of(both), NN)
        put(ky, result[:, :LANES])
        put(ky + 1, result[:, LANES:])

    unrolled = 4

    def body(m, carry):
        for v in range(unrolled):
            pair(2 * (unrolled * m + v))
        return carry

    lax.fori_loop(0, count // (2 * unrolled), body, 0)
    for ky in range(count // (2 * unrolled) * 2 * unrolled, count - 1, 2):
        pair(ky)
    if count % 2:
        put(count - 1, product3(table, halves_of(lines(count - 1)), NN))


def back_x_depth(count):
    sines = -(-count // 8) * 8
    return sines, (2 * sines // 8 | 1) * 8


def back_along_x(w, count):
    sources, _, rows, _ = w.shape
    high, low = back_x_table()
    sines, depth = back_x_depth(count)
    side = lambda s: pl.BlockSpec(
        (sources, None, rows, LANES), lambda i: (0, s, 0, 0), pipeline_mode=pl.Buffered(1)
    )
    return pl.pallas_call(
        lambda *refs: back_x_kernel(count, depth, sines, *refs),
        grid=(1,),
        in_specs=[side(0), side(1), whole(high), whole(low)],
        out_specs=pl.BlockSpec((KEPT * depth, LANES), lambda i: (0, 0)),
        out_shape=jax.ShapeDtypeStruct((KEPT * depth, LANES), f32),
        cost_estimate=pl.CostEstimate(
            flops=6 * count * 256 * 256 * LANES, bytes_accessed=10 * 1024 * 1024, transcendentals=0
        ),
        compiler_params=pltpu.CompilerParams(vmem_limit_bytes=24 * MIB),
        interpret=INTERPRET,
        name="back_along_x",
    )(w, w, high, low)


def gather_back_along_x(blocks, own, count, after):
    _, rows, _ = blocks[0].shape
    high, low = back_x_table()
    sines, depth = back_x_depth(count)
    return pl.pallas_call(
        lambda *refs: gather_back_x_kernel(len(blocks), count, depth, sines, *refs),
        grid=(1,),
        in_specs=[pl.BlockSpec(memory_space=pltpu.SMEM)] + [whole(a) for a in (*blocks, high, low)]
        + [anywhere] * len(after),
        out_specs=pl.BlockSpec((KEPT * depth, LANES), lambda i: (0, 0)),
        out_shape=jax.ShapeDtypeStruct((KEPT * depth, LANES), f32),
        scratch_shapes=[pltpu.VMEM((2, len(blocks) * rows, LANES), f32)],
        cost_estimate=pl.CostEstimate(
            flops=6 * count * 256 * 256 * LANES, bytes_accessed=10 * 1024 * 1024, transcendentals=0
        ),
        compiler_params=pltpu.CompilerParams(vmem_limit_bytes=24 * MIB),
        interpret=INTERPRET,
        name="gather_back_along_x",
    )(own, *blocks, high, low, *after)


def back_y_table(first, chunks):
    tables = []
    y = np.arange(LANES)
    for count in chunks:
        sines, depth = back_x_depth(count)
        ky = np.arange(first, first + count)
        angle = np_angle(ky, y)
        table = np.zeros((depth, 2 * LANES))
        table[:count, :LANES] = np_twice(ky)[:, None] * np.cos(angle)
        table[sines : sines + count, LANES:] = np_twice(ky)[:, None] * np.sin(angle)
        tables.append(table)
        first += count
    return table_halves(np.concatenate(tables, axis=0))


X_STEP = 16


def turned_lines(parts, table):
    result = product3(halves_of(jnp.concatenate(parts, axis=0).T), table, NN)
    cosines, sines = result[:, :LANES], result[:, LANES:]
    return cosines - sines, cosines + sines


def packed_lines(lines, table):
    high = lines.astype(bf16).astype(f32)
    stacked = jnp.concatenate([high, high, lines - high], axis=0)
    result = product(stacked.T.astype(bf16), table, NN)
    cosines, sines = result[:, :LANES], result[:, LANES:]
    return cosines - sines, cosines + sines


def partial_back_y_kernel(depths, *refs):
    blocks, (high_ref, low_ref, minus_ref, plus_ref) = refs[:-4], refs[-4:]
    table = (high_ref[...], low_ref[...])
    for s in range(minus_ref.shape[0]):
        lines = [r[s * d : (s + 1) * d, :] for r, d in zip(blocks, depths)]
        minus_ref[s], plus_ref[s] = turned_lines(lines, table)


def partial_back_along_y(parts, chunks):
    high, low = back_y_table(0, chunks)
    depths = tuple(back_x_depth(c)[1] for c in chunks)
    step = 8
    line = jax.ShapeDtypeStruct((KEPT, LANES, LANES), f32)
    return pl.pallas_call(
        lambda *refs: partial_back_y_kernel(depths, *refs),
        grid=(-(-KEPT // step),),
        in_specs=[pl.BlockSpec((step * d, LANES), lambda i: (i, 0)) for d in depths] + [whole(high), whole(low)],
        out_specs=[pl.BlockSpec((step, LANES, LANES), lambda i: (i, 0, 0))] * 2,
        out_shape=[line, line],
        cost_estimate=pl.CostEstimate(
            flops=6 * KEPT * 128 * 256 * 256, bytes_accessed=24 * MIB, transcendentals=0
        ),
        interpret=INTERPRET,
        name="partial_back_along_y",
    )(*parts, high, low)


def back_y_kernel(depth, *refs):
    halves, heads, zeroth = refs[:3], refs[3:6], refs[6:9]
    table_ref, own_ref, out_ref, minus_ref, plus_ref = refs[9:]
    step, side = pl.program_id(0), pl.program_id(1)
    table = table_ref[...]
    lane = lax.broadcasted_iota(jnp.int32, (LANES, LANES), 1)
    turned_lane = (LANES // 2 - lane) & (LANES - 1)
    ring = 2 * X_STEP

    def fill(source, s, line):
        z_ref, early_minus_ref, early_plus_ref = source
        minus, plus = packed_lines(z_ref[s * depth : (s + 1) * depth, :], table)
        slot = line & (ring - 1)
        minus_ref[slot] = minus + early_minus_ref[s]
        plus_ref[slot] = plus + early_plus_ref[s]

    @pl.when((step == 0) & (side == 0))
    def _():
        fill(zeroth, 0, step)
        for s in range(X_STEP // 2):
            fill(heads, s, step + 1 + s)

    half = jnp.minimum(2 * step + 1 + side, 2 * HALF_L // X_STEP - 1)
    for s in range(X_STEP // 2):
        fill(halves, s, half * (X_STEP // 2) + 1 + s)

    def emit(near_ref, far_ref, offsets):
        slots = [(step * X_STEP + s) & (ring - 1) for s in offsets]
        for u in range(X_STEP // 2):
            even, odd = slots[2 * u], slots[2 * u + 1]
            near = near_ref[even]
            far = gathered(far_ref[even], turned_lane)
            near_odd = lane_swap(near_ref[odd])
            far_odd = lane_swap(gathered(far_ref[odd], turned_lane))
            tiles = (
                jnp.where(lane <= HALF_L, near, far),
                jnp.where(lane < LANES // 2, far, near_odd),
                jnp.where(lane <= HALF_L - LANES // 2, near_odd, far_odd),
            )
            for i, w in enumerate(tiles):
                lanes = slice(u * PAIR + i * LANES, u * PAIR + (i + 1) * LANES)
                out_ref[:, lanes] = -own_ref[:, lanes] * w

    @pl.when(side == 0)
    def _():
        emit(minus_ref, plus_ref, range(X_STEP))

    @pl.when(side == 1)
    def _():
        emit(plus_ref, minus_ref, range(X_STEP, 0, -1))


def back_along_y(propagator, early, last, first, count):
    slab, sites = propagator.shape
    high, low = back_y_table(first, [count])
    table = jnp.concatenate([high, low, high], axis=0)
    depth = back_x_depth(count)[1]
    width = X_STEP * L
    steps = HALF_L // X_STEP
    half = X_STEP // 2
    moving = pl.BlockSpec((slab, width), lambda i, j: (0, jnp.where(j == 0, i, 2 * steps - 1 - i)))

    def lines(size, index):
        return [pl.BlockSpec((size * depth, LANES), lambda i, j: (index(i, j), 0))] + [
            pl.BlockSpec((size, LANES, LANES), lambda i, j: (index(i, j), 0, 0))
        ] * 2

    sources = (last, *early)
    return pl.pallas_call(
        lambda *refs: back_y_kernel(depth, *refs),
        grid=(steps, 2),
        in_specs=lines(half, lambda i, j: jnp.minimum(2 * i + 1 + j, 2 * steps - 1))
        + lines(half, lambda i, j: 0)
        + lines(1, lambda i, j: HALF_L)
        + [whole(table), moving],
        out_specs=moving,
        out_shape=jax.ShapeDtypeStruct((slab, sites), f32),
        scratch_shapes=[pltpu.VMEM((2 * X_STEP, LANES, LANES), f32)] * 2,
        cost_estimate=pl.CostEstimate(
            flops=6 * KEPT * 128 * 256 * 256, bytes_accessed=2 * propagator.size * 4, transcendentals=0
        ),
        interpret=INTERPRET,
        name="back_along_y",
    )(*sources, *sources, *sources, table, propagator)


CUTS = (0, 40, KEPT // 2 + 1)
CHUNKS = ((32, 8, 64, False), (33, 12, 104, True), (32, 8, 64, False))


def token(x):
    return lax.slice(x.reshape(-1, LANES), (0, 0), (8, LANES))


def chunk_firsts():
    return [sum(c[0] for c in CHUNKS[:i]) for i in range(len(CHUNKS))]


def pick_kernel(own_ref, w_ref, *refs):
    slabs = w_ref.shape[0]
    for k, out_ref in enumerate(refs[-slabs:]):
        out_ref[...] = w_ref[own_ref[0] ^ k]


def picked(w, own, after):
    shape = w.shape[1:]
    return list(
        pl.pallas_call(
            pick_kernel,
            grid=(1,),
            in_specs=[pl.BlockSpec(memory_space=pltpu.SMEM), whole(w)] + [anywhere] * len(after),
            out_specs=[pl.BlockSpec(shape, lambda i: (0, 0, 0))] * w.shape[0],
            out_shape=[jax.ShapeDtypeStruct(shape, f32)] * w.shape[0],
            cost_estimate=pl.CostEstimate(flops=0, bytes_accessed=8 * w.size, transcendentals=0),
            compiler_params=pltpu.CompilerParams(vmem_limit_bytes=16 * MIB),
            interpret=INTERPRET,
            name="picked",
        )(own, w, *after)
    )


def frequency_tables(points, slab):
    half = slab // 2
    quarter = points // 4
    slot = lax.optimization_barrier(jnp.arange(quarter, dtype=jnp.int32))
    count = lax.optimization_barrier(jnp.arange(NF // 2, dtype=jnp.int32))
    held = slot // half * slab + slot % half
    tables = []
    for times, turned in ((held, False), (slot, True)):
        for parity in (0, 1):
            n = 2 * count + parity
            a, b = (n[:, None], times[None, :]) if turned else (n[None, :], times[:, None])
            phase = a * (2 * b + 1) % (2 * points)
            table = jnp.cos(jnp.pi * phase.astype(f32) / points) * (2.0 / math.sqrt(points))
            high = lax.reduce_precision(table, 8, 7)
            tables += [high.astype(bf16), (table - high).astype(bf16)]
    return tables


def with_kernels(propagator, onsite_coupling, neighbour_strength):
    devices = lax.axis_size("tau")
    me = lax.axis_index("tau")
    slab, _ = propagator.shape
    half = slab // 2

    partner = [(d, devices - 1 - d) for d in range(devices)]
    tables = frequency_tables(slab * devices, slab)
    lines = None
    for first, last in zip(CUTS[:-1], CUTS[1:]):
        mirror = lax.ppermute(propagator[half:, first * PAIR : last * PAIR], "tau", partner)
        lines = bubble_along_y(propagator, mirror, first, last - first, lines, [] if first else tables)

    sides = devices // 2
    own = (me % sides)[None].astype(jnp.int32)
    sign = jnp.where(me < sides, 1.0, -1.0)[None].astype(f32)
    firsts = chunk_firsts()
    moved, turned = [], []
    for i, (first, (count, span, block, shared)) in enumerate(zip(firsts, CHUNKS)):
        owners = sides if shared else devices
        rows = -(-count * HALF_L // (8 * owners)) * 8
        pol_mom = along_x([lines], first, span, rows * owners, devices // owners, [token(m) for m in moved[-1:]] + [token(w) for w in turned[: max(i - 1, 0)]])
        moved.append(pol_mom)
        pol_mom = pol_mom.reshape(devices, rows, LANES)
        by_momentum = lax.all_to_all(pol_mom, "tau", split_axis=0, concat_axis=0, tiled=True)
        row = me % owners * rows + jnp.arange(rows, dtype=jnp.int32)
        bare = jnp.stack(
            [
                bare_potential(
                    row % HALF_L + HALF_L * side, first + row // HALF_L, onsite_coupling[0], neighbour_strength[0]
                )
                for side in (0, 1)
            ]
        )[:, :, None]
        turned.append(through_frequencies(by_momentum, bare, tables, block, sign, not shared, [token(w) for w in turned[-1:]]))

    def exchanged(blocks):
        for k in range(1, len(blocks)):
            blocks[k] = lax.ppermute(blocks[k], "tau", [(d, d ^ k) for d in range(devices)])
        return blocks

    returned = []
    counts = [c[0] for c in CHUNKS]
    for first, (count, _, _, shared), w in zip(firsts, CHUNKS, turned):
        if shared:
            blocks = exchanged(picked(w, own, []))
            returned.append(gather_back_along_x(blocks, own, count, []))
        elif w is turned[-1]:
            place = me[None].astype(jnp.int32)
            blocks = exchanged(picked(w, place, []))
            early = partial_back_along_y(returned, counts[:-1])
            last = gather_back_along_x(blocks, place, count, [token(e) for e in early])
        else:
            w = lax.all_to_all(w, "tau", split_axis=0, concat_axis=0, tiled=True)
            returned.append(back_along_x(w, count))
    return back_along_y(propagator, early, last, firsts[-1], counts[-1])


def per_device(propagator, onsite_coupling, neighbour_strength):
    slab, sites = propagator.shape
    devices = lax.axis_size("tau")
    fits = slab == LANES and sites == L * L and 4 * NF == 2 * slab * devices and devices & (devices - 1) == 0
    run = with_kernels if fits else plain
    return run(propagator, onsite_coupling, neighbour_strength)


def solution(mesh):
    in_specs = (P(("grp", "tau"), None), P("grp"), P("grp"))
    out_specs = P(("grp", "tau"), None)
    return jax.shard_map(
        per_device, mesh=mesh, in_specs=in_specs, out_specs=out_specs, check_vma=False
    )
```
